128 devices in a mesh: row: 8 (over x_hi, z), col: 16 (over y, x_lo, core).
Axes of the slice: x: 4 (x_hi: 2, x_lo: 2; x = x_hi * 2 + x_lo), y: 4, z: 4, core: 2. Of those that a mesh axis runs over, the one named last changes fastest.
Arguments:
- query_vectors: bfloat16 [4096, 16, 128], P('col', 'row'), may hold values from -68 to 68
- key_vectors: bfloat16 [4096, 16, 128], P('col', 'row'), may hold values from -6 to 6
- value_vectors: bfloat16 [4096, 16, 128], P('col', 'row'), may hold values from -6 to 6
- gate_logits: bfloat16 [4096, 16, 128], P('col', 'row'), may hold values from -6 to 6
- cotangent: bfloat16 [4096, 16, 128], P('col', 'row'), may hold values from -6 to 6
- pair_bias: bfloat16 [32, 4, 128, 16, 128], P('col'), may hold values from -6 to 6
- block_table: int32 [32, 16], P('col'), may hold values from 0 to 31, as said below
- valid_counts: int32 [32], P('col'), may hold values from 1 to 16
Outputs:
- query_grad: bfloat16 [4096, 16, 128], P('col', 'row')
- key_grad: bfloat16 [4096, 16, 128], P('col', 'row')
- value_grad: bfloat16 [4096, 16, 128], P('col', 'row')
- gate_grad: bfloat16 [4096, 16, 128], P('col', 'row')
- bias_grad: bfloat16 [32, 4, 128, 16, 128], P('col', None, None, 'row')
The draws below stay inside these ranges and needn't reach their ends.
Inputs may be any that keep to these rules, and one draw needn't show every extreme that they name: `block_table`: each row holds 16 distinct block numbers; its first entry is the row's own block number.
All inputs are finite; a program needn't handle non-finite values.
Results may differ from the reference program's by a relative error of at most 0.03.
Values may be sent and summed in bfloat16 or wider, within the bound.
No kernel may reach another device: no remote copies, remote signals or barrier semaphores. Data moves between devices by JAX's collectives and lax.ppermute only.
A program may use at most 128 MiB of HBM per device.

```python
import jax
import jax.numpy as jnp
from jax import lax

C = 128
H = 4
DH = 32
BS = 128
TAB = 16
I_DEV = 2
JB_DEV = 2
N = 4096
NB = 32
ROWS = 16
N_ROW = 8
N_COL = 16


def drawn_keys(key):
    base = jax.random.fold_in(key, 101)
    drawn = jnp.clip(jax.random.normal(base, (N, ROWS, C), jnp.float32), -6.0, 6.0)
    return drawn


def draw_key_vectors(key, part):
    drawn = drawn_keys(key)
    return drawn.astype(jnp.bfloat16)


def draw_query_vectors(key, part):
    noise_key = jax.random.fold_in(key, 103)
    result = jnp.clip(jax.random.normal(noise_key, (N, ROWS, C), jnp.float32), -6.0, 6.0)
    return result.astype(jnp.bfloat16)


def draw_block_table(key, part):
    row_keys = jax.random.split(jax.random.fold_in(key, 201), NB)
    shifts = jax.vmap(lambda single: jax.random.permutation(single, NB - 1))(row_keys)[:, :TAB - 1] + 1
    own = jnp.arange(NB, dtype=jnp.int32)[:, None]
    return jnp.concatenate([own, (own + shifts) % NB], axis=1).astype(jnp.int32)


def draw_valid_counts(key, part):
    counts = jax.random.randint(jax.random.fold_in(key, 301), (NB,), 1, TAB + 1)
    fullest = jax.random.randint(jax.random.fold_in(key, 302), (), 0, NB)
    shortest = (fullest + 1 + jax.random.randint(jax.random.fold_in(key, 303), (), 0, NB - 1)) % NB
    position = jnp.arange(NB)
    counts = jnp.where(position == fullest, TAB, counts)
    counts = jnp.where(position == shortest, 1, counts)
    return counts.astype(jnp.int32)


def level_of(key, shape, cuts, least, largest):
    def one(dim, blocks):
        heights = jax.random.uniform(jax.random.fold_in(jax.random.fold_in(key, 6), dim), (blocks,), jnp.float32, least / len(cuts), largest / len(cuts))
        return jnp.repeat(jnp.exp(heights), shape[dim] // blocks).reshape((-1,) + (1,) * (len(shape) - dim - 1))

    gain = one(*cuts[0])
    for cut in cuts[1:]:
        gain = gain * one(*cut)
    return gain


def centred(own_key, dims, spread, bound, pieces=(), held_as=jnp.bfloat16):
    values = jax.random.normal(own_key, dims, jnp.float32) * spread
    if len(pieces) > 0:
        values = level_of(own_key, dims, pieces, -0.22, 0.18) * values
    return jnp.clip(values, min=-bound, max=bound).astype(held_as)


def setup_inputs(seed: int = 0) -> dict:
    key_list = jax.random.split(jax.random.key(seed), 9)
    return {
        "query_vectors": draw_query_vectors(jax.random.fold_in(key_list[8], 71), 0),
        "key_vectors": draw_key_vectors(jax.random.fold_in(key_list[8], 71), 0),
        "value_vectors": centred(key_list[2], (N, ROWS, C), 1.0, 6.0, ((0, 16), (1, 8))),
        "gate_logits": centred(key_list[3], (N, ROWS, C), 1.5, 6.0, ((0, 16), (1, 8))),
        "cotangent": centred(key_list[4], (N, ROWS, C), 1.0, 6.0, ((0, 16), (1, 8))),
        "pair_bias": centred(key_list[5], (NB, H, BS, TAB, BS), 1.0, 6.0, ((0, 16),)),
        "block_table": draw_block_table(jax.random.fold_in(key_list[8], 71), 0),
        "valid_counts": draw_valid_counts(jax.random.fold_in(key_list[8], 71), 0),
    }


def block_terms(query_blk, gate_blk, upstream_blk, key_blk, value_blk, bias_blk, valid_count):
    row_count = query_blk.shape[1]
    extent = key_blk.shape[0]
    scale = DH ** -0.5
    query_four = query_blk.astype(jnp.float32).reshape(BS, row_count, H, DH)
    key_four = key_blk.astype(jnp.float32).reshape(extent, row_count, H, DH)
    value_four = value_blk.astype(jnp.float32).reshape(extent, row_count, H, DH)
    scores = jnp.einsum("qihd,kihd->ihqk", query_four, key_four) * scale
    scores = scores + bias_blk.astype(jnp.float32).reshape(H, BS, extent)[None]
    valid = (jnp.arange(extent) // BS) < valid_count
    scores = jnp.where(valid, scores, -jnp.inf)
    maxima = jnp.max(scores, axis=-1, keepdims=True)
    exponent = jnp.exp(scores - maxima)
    probability = exponent / jnp.sum(exponent, axis=-1, keepdims=True)
    weights = lax.optimization_barrier(probability.astype(jnp.bfloat16)).astype(jnp.float32)
    attended = jnp.einsum("ihqk,kihd->qihd", weights, value_four)
    opened = jax.nn.sigmoid(gate_blk.astype(jnp.float32)).reshape(BS, row_count, H, DH)
    upstream = upstream_blk.astype(jnp.float32).reshape(BS, row_count, H, DH)
    gate_grad = (upstream * attended * opened * (1.0 - opened)).reshape(BS, row_count, H * DH).astype(jnp.bfloat16)
    core_grad = lax.optimization_barrier((upstream * opened).astype(jnp.bfloat16)).astype(jnp.float32)
    offset = jnp.einsum("qihd,qihd->ihq", core_grad, attended)[..., None]
    weight_grad = jnp.einsum("qihd,kihd->ihqk", core_grad, value_four)
    score_grad = probability * (weight_grad - offset)
    score_half = lax.optimization_barrier(score_grad.astype(jnp.bfloat16)).astype(jnp.float32)
    query_grad = (jnp.einsum("ihqk,kihd->qihd", score_half, key_four) * scale).reshape(BS, row_count, H * DH).astype(jnp.bfloat16)
    key_term = jnp.einsum("ihqk,qihd->kihd", score_half, query_four) * scale
    value_term = jnp.einsum("ihqk,qihd->kihd", weights, core_grad)
    return query_grad, gate_grad, key_term.reshape(extent, row_count, H * DH), value_term.reshape(extent, row_count, H * DH), score_grad


def reference(query_vectors, key_vectors, value_vectors, gate_logits, cotangent, pair_bias, block_table, valid_counts):
    row_count = query_vectors.shape[1]
    key_blocks = key_vectors.reshape(NB, BS, row_count, C)
    value_blocks = value_vectors.reshape(NB, BS, row_count, C)

    def group_step(carry, group):
        key_total, value_total = carry
        key_acc = jnp.zeros((NB, BS, row_count, C), jnp.float32)
        value_acc = jnp.zeros((NB, BS, row_count, C), jnp.float32)
        query_parts = []
        gate_parts = []
        bias_parts = []
        for local in range(JB_DEV):
            block = (group * JB_DEV + local).astype(jnp.int32)
            start = (block * BS).astype(jnp.int32)
            query_blk = lax.dynamic_slice_in_dim(query_vectors, start, BS, 0)
            gate_blk = lax.dynamic_slice_in_dim(gate_logits, start, BS, 0)
            upstream_blk = lax.dynamic_slice_in_dim(cotangent, start, BS, 0)
            block_ids = lax.dynamic_index_in_dim(block_table, block, 0, keepdims=False).astype(jnp.int32)
            valid_count = lax.dynamic_index_in_dim(valid_counts, block, 0, keepdims=False)
            bias_blk = lax.dynamic_index_in_dim(pair_bias, block, 0, keepdims=False)
            key_blk = jnp.take(key_blocks, block_ids, axis=0).reshape(TAB * BS, row_count, C)
            value_blk = jnp.take(value_blocks, block_ids, axis=0).reshape(TAB * BS, row_count, C)
            query_grad, gate_grad, key_term, value_term, score_grad = block_terms(query_blk, gate_blk, upstream_blk, key_blk, value_blk, bias_blk, valid_count)
            key_acc = key_acc.at[block_ids].add(key_term.reshape(TAB, BS, row_count, C))
            value_acc = value_acc.at[block_ids].add(value_term.reshape(TAB, BS, row_count, C))
            row_partial = score_grad.reshape(N_ROW, I_DEV, H, BS, TAB * BS).sum(axis=1)
            row_partial = lax.optimization_barrier(row_partial.astype(jnp.bfloat16)).astype(jnp.float32)
            bias_parts.append(row_partial.sum(axis=0).reshape(H, BS, TAB, BS).astype(jnp.bfloat16))
            query_parts.append(query_grad)
            gate_parts.append(gate_grad)
        key_total = key_total + lax.optimization_barrier(key_acc.astype(jnp.bfloat16)).astype(jnp.float32)
        value_total = value_total + lax.optimization_barrier(value_acc.astype(jnp.bfloat16)).astype(jnp.float32)
        outputs = (jnp.concatenate(query_parts, 0), jnp.concatenate(gate_parts, 0), jnp.stack(bias_parts, 0))
        return (key_total, value_total), outputs

    initial = (jnp.zeros((NB, BS, row_count, C), jnp.float32), jnp.zeros((NB, BS, row_count, C), jnp.float32))
    groups = jnp.arange(N_COL, dtype=jnp.int32)
    totals, stacked = lax.scan(group_step, initial, groups)
    key_grad = totals[0].reshape(N, row_count, C).astype(jnp.bfloat16)
    value_grad = totals[1].reshape(N, row_count, C).astype(jnp.bfloat16)
    query_grad = stacked[0].reshape(N, row_count, C)
    gate_grad = stacked[1].reshape(N, row_count, C)
    bias_grad = stacked[2].reshape(NB, H, BS, TAB, BS)
    return query_grad, key_grad, value_grad, gate_grad, bias_grad
```

```python
import math

import jax
import jax.numpy as jnp
from jax import lax
from jax.experimental import pallas as pl
from jax.experimental.pallas import tpu as pltpu
from jax.sharding import PartitionSpec as P

H = 4
DH = 32
BS = 128
TAB = 16
SCALE = DH**-0.5
LOG2E = math.log2(math.e)
F32 = jnp.float32
BF = jnp.bfloat16
NT = (((1,), (1,)), ((), ()))
NN = (((1,), (0,)), ((), ()))


def dot(a, b, dims):
    return lax.dot_general(a, b, dims, preferred_element_type=F32)


def attend_kernel(first, *refs):
    if first:
        (idx, cnt, chk, q, gate, cot, kv, bias, dq, gg, bg, dkv, *scratch) = refs
    else:
        (idx, cnt, chk, q, gate, cot, kv, bias, prev, dq, gg, bg, dkv, *scratch) = refs
    s_ref, e_ref, m_ref, l_ref, o_ref, off_ref, qm, qt, dom, domt, acc = scratch
    n = cnt[0]
    pairs = (n + 1) // 2
    lane = lax.broadcasted_iota(jnp.int32, (BS, BS), 1) // DH
    for i in range(2):
        qi = q[i]
        for h in range(H):
            r = slice(h * BS, (h + 1) * BS)
            v = jnp.where(lane == h, qi, jnp.zeros_like(qi))
            qm[i, r, :] = v
            qt[i, :, r] = v.T
    m_ref[...] = jnp.full(m_ref.shape, -jnp.inf, F32)
    l_ref[...] = jnp.zeros(l_ref.shape, F32)
    o_ref[...] = jnp.zeros(o_ref.shape, F32)
    if first:
        acc[...] = jnp.zeros(acc.shape, F32)
    else:

        def load(b, carry):
            acc[b] = prev[b].astype(F32)
            return carry

        lax.fori_loop(0, 32, load, 0)
    bg[...] = jnp.zeros(bg.shape, BF)

    def both(p, i, w):
        return jnp.concatenate([kv[idx[2 * p], i, w], kv[idx[2 * p + 1], i, w]], 0)

    def score(p, carry):
        for h in range(H):
            r = slice(h * BS, (h + 1) * BS)
            b0 = bias[0, h, 2 * p].astype(F32) * LOG2E
            b1 = bias[0, h, 2 * p + 1].astype(F32) * LOG2E
            b1 = jnp.where(2 * p + 1 < n, b1, -1e30)
            for i in range(2):
                s = dot(qm[i, r, :], both(p, i, 0), NT) * (SCALE * LOG2E)
                s0 = s[:, :BS] + b0
                s1 = s[:, BS:] + b1
                s_ref[p, i, r, :BS] = s0
                s_ref[p, i, r, BS:] = s1
                m_ref[i, r, :] = jnp.maximum(m_ref[i, r, :], jnp.maximum(s0, s1))
        return carry

    lax.fori_loop(0, pairs, score, 0)
    for i in range(2):
        m_ref[i] = jnp.broadcast_to(jnp.max(m_ref[i], axis=1, keepdims=True), (H * BS, BS))

    def attend(p, carry):
        for i in range(2):
            v2 = both(p, i, 1)
            for h in range(H):
                r = slice(h * BS, (h + 1) * BS)
                m = m_ref[i, r, :]
                e0 = jnp.exp2(s_ref[p, i, r, :BS] - m)
                e1 = jnp.exp2(s_ref[p, i, r, BS:] - m)
                l_ref[i, r, :] += e0 + e1
                e = jnp.concatenate([e0.astype(BF), e1.astype(BF)], 1)
                e_ref[p, i, r, :] = e
                o_ref[i, r, :] += dot(e, v2, NN)
        return carry

    lax.fori_loop(0, pairs, attend, 0)
    for i in range(2):
        att = jnp.zeros((BS, BS), F32)
        inv = []
        for h in range(H):
            r = slice(h * BS, (h + 1) * BS)
            inv.append(1.0 / jnp.sum(l_ref[i, r, :], axis=1, keepdims=True))
            att = jnp.where(lane == h, o_ref[i, r, :] * inv[h], att)
        c = cot[i].astype(F32)
        opened = 1.0 / (1.0 + jnp.exp(-gate[i].astype(F32)))
        gg[i] = (c * att * opened * (1.0 - opened)).astype(BF)
        core = (c * opened).astype(BF).astype(F32)
        for h in range(H):
            r = slice(h * BS, (h + 1) * BS)
            d = jnp.where(lane == h, core * inv[h], 0.0).astype(BF)
            dom[i, r, :] = d
            domt[i, :, r] = d.T
            off = jnp.sum(d.astype(F32) * att, axis=1, keepdims=True)
            off_ref[i, r, :] = jnp.broadcast_to(off, (BS, BS))
    o_ref[...] = jnp.zeros(o_ref.shape, F32)

    def backward(p, carry):
        a0 = idx[2 * p]
        a1 = idx[2 * p + 1]
        ch = chk[p]
        total = [None] * H
        for i in range(2):
            k2 = both(p, i, 0)
            v2 = both(p, i, 1)
            halves = []
            for h in range(H):
                r = slice(h * BS, (h + 1) * BS)
                off = off_ref[i, r, :]
                wg = dot(dom[i, r, :], v2, NT)
                ds = e_ref[p, i, r, :].astype(F32) * (wg - jnp.concatenate([off, off], 1))
                if i == 0:
                    total[h] = ds
                else:
                    b = (total[h] + ds).astype(BF)
                    bg[ch, h, 0] = b[:, :BS]
                    bg[ch, h, 1] = b[:, BS:]
                half = ds.astype(BF)
                halves.append(half)
                o_ref[i, r, :] += dot(half, k2, NN)
            dk = dot(qt[i], jnp.concatenate(halves, 0), NN)
            dv = dot(domt[i], e_ref[p, i], NN)
            acc[a0, i, 0] += dk[:, :BS]
            acc[a1, i, 0] += dk[:, BS:]
            acc[a0, i, 1] += dv[:, :BS]
            acc[a1, i, 1] += dv[:, BS:]
        return carry

    lax.fori_loop(0, pairs, backward, 0)
    for i in range(2):
        x = jnp.zeros((BS, BS), F32)
        for h in range(H):
            x = jnp.where(lane == h, o_ref[i, h * BS : (h + 1) * BS, :], x)
        dq[i] = (x * SCALE).astype(BF)

    def store(b, carry):
        dkv[b] = acc[b].astype(BF)
        return carry

    lax.fori_loop(0, 32, store, 0)


def attend_block(local, idx, cnt, chk, q, gate, cot, kv, bias, prev):
    first = prev is None
    smem = pl.BlockSpec(memory_space=pltpu.SMEM)
    vmem = pl.BlockSpec(memory_space=pltpu.VMEM)
    bias_spec = pl.BlockSpec((1, H, TAB, BS, BS), lambda g: (local, 0, 0, 0, 0))
    whole = lambda *s: pl.BlockSpec(s, lambda g: (0,) * len(s))
    args = [idx, cnt, chk, q, gate, cot, kv, bias]
    specs = [smem] * 3 + [whole(2, BS, BS)] * 3 + [whole(32, 2, 2, BS, BS), bias_spec]
    if not first:
        args.append(prev)
        specs.append(whole(32, 2, 2, BS, BS))

    def kernel(*refs):
        attend_kernel(first, *refs)

    shapes = ((2, BS, BS), (2, BS, BS), (8, H, 2, BS, BS), (32, 2, 2, BS, BS))
    return pl.pallas_call(
        kernel,
        grid=(1,),
        out_shape=tuple(jax.ShapeDtypeStruct(s, BF) for s in shapes),
        in_specs=specs,
        out_specs=tuple(whole(*s) for s in shapes),
        scratch_shapes=[
            pltpu.VMEM((8, 2, H * BS, 2 * BS), F32),
            pltpu.VMEM((8, 2, H * BS, 2 * BS), BF),
            pltpu.VMEM((2, H * BS, BS), F32),
            pltpu.VMEM((2, H * BS, BS), F32),
            pltpu.VMEM((2, H * BS, BS), F32),
            pltpu.VMEM((2, H * BS, BS), F32),
            pltpu.VMEM((2, H * BS, BS), BF),
            pltpu.VMEM((2, BS, H * BS), BF),
            pltpu.VMEM((2, H * BS, BS), BF),
            pltpu.VMEM((2, BS, H * BS), BF),
            pltpu.VMEM((32, 2, 2, BS, BS), F32),
        ],
        compiler_params=pltpu.CompilerParams(vmem_limit_bytes=60 << 20),
        cost_estimate=pl.CostEstimate(
            flops=10_000_000_000, bytes_accessed=24 << 20, transcendentals=4 << 20
        ),
        name="attend_block",
    )(*args)


def body(
    query_vectors,
    key_vectors,
    value_vectors,
    gate_logits,
    cotangent,
    pair_bias,
    block_table,
    valid_counts,
):
    col = lax.axis_index("col")
    row = lax.axis_index("row")
    y, xl, core = col // 4, (col // 2) % 2, col % 2
    xh, z = row // 4, row % 4

    def to_col(x, dy, dx, dc):
        pairs = []
        for s in range(16):
            sy, sx, sc = s // 4, (s // 2) % 2, s % 2
            pairs.append((s, ((sy + dy) % 4) * 4 + (sx ^ dx) * 2 + (sc ^ dc)))
        return lax.ppermute(x, "col", pairs)

    def to_row(x, dx, dz):
        pairs = [(s, ((s // 4) ^ dx) * 4 + (s % 4 + dz) % 4) for s in range(8)]
        return lax.ppermute(x, "row", pairs)

    def blocks(x):
        return x.reshape(2, BS, 2, BS).transpose(0, 2, 1, 3)

    shard = jnp.stack([blocks(key_vectors), blocks(value_vectors)], 2)
    pieces = []
    for dy in range(4):
        for dx in range(2):
            pieces.append(to_col(shard, (4 - dy) % 4, dx, 0) if dy + dx else shard)
    same = jnp.concatenate(pieces, 0)
    other = to_col(same, 0, 0, 1)
    kv = jnp.concatenate([same, other], 0)

    ids = block_table
    owner = ids // 2
    piece = ((owner % 2) ^ core) * 8 + ((owner // 4 - y) % 4) * 2 + (((owner // 2) % 2) ^ xl)
    idx = piece * 2 + ids % 2
    dest = jnp.arange(8, dtype=jnp.int32)
    far = (dest // 4) ^ xh
    turn = (dest % 4 - z) % 4
    chunk_a = far * 4 + turn
    chunk_b = turn * 2 + far

    bias = pair_bias.transpose(0, 1, 3, 2, 4)
    q, gate, cot = blocks(query_vectors), blocks(gate_logits), blocks(cotangent)
    counts = valid_counts.reshape(2, 1)

    dq0, gg0, bg0, dkv0 = attend_block(
        0, idx[0], counts[0], chunk_a, q[0], gate[0], cot[0], kv, bias, None
    )
    bg0 = bg0.reshape(2, 4, H, 2, BS, BS)
    bg0_far = to_row(bg0[1], 1, 0)
    dq1, gg1, bg1, dkv = attend_block(
        1, idx[1], counts[1], chunk_b, q[1], gate[1], cot[1], kv, bias, dkv0
    )
    bg1 = bg1.reshape(4, 2, H, 2, BS, BS)

    def plus(*terms):
        total = terms[0].astype(F32)
        for t in terms[1:]:
            total = total + t.astype(F32)
        return total.astype(BF)

    dkv = dkv.reshape(2, 4, 2, 2, 2, 2, BS, BS)
    mine = plus(dkv[0], to_col(dkv[1], 0, 0, 1))
    part = plus(mine[0], *[to_col(mine[dy], dy, 0, 0) for dy in range(1, 4)])
    own = part[0].astype(F32) + to_col(part[1], 0, 1, 0).astype(F32)

    bg0 = plus(bg0[0], bg0_far)
    bias0 = plus(bg0[0], *[to_row(bg0[dz], 0, dz) for dz in range(1, 4)])
    bg1 = plus(bg1[0], *[to_row(bg1[dz], 0, dz) for dz in range(1, 4)])
    bias1 = plus(bg1[0], to_row(bg1[1], 1, 0))
    bias_grad = jnp.stack([bias0, bias1], 0).transpose(0, 1, 3, 2, 4)

    def rows(x):
        return x.transpose(0, 3, 1, 2).reshape(2 * BS, 2, BS).astype(BF)

    key_grad = rows(own[:, :, 0] * SCALE)
    value_grad = rows(own[:, :, 1])

    def back(a, b):
        return jnp.stack([a, b], 0).transpose(0, 2, 1, 3).reshape(2 * BS, 2, BS)

    return back(dq0, dq1), key_grad, value_grad, back(gg0, gg1), bias_grad


def solution(mesh):
    return jax.shard_map(
        body,
        mesh=mesh,
        in_specs=(
            P("col", "row", None),
            P("col", "row", None),
            P("col", "row", None),
            P("col", "row", None),
            P("col", "row", None),
            P("col", None, None, None, None),
            P("col", None),
            P("col"),
        ),
        out_specs=(
            P("col", "row", None),
            P("col", "row", None),
            P("col", "row", None),
            P("col", "row", None),
            P("col", None, None, "row", None),
        ),
        check_vma=False,
    )
```

```python
import math

import jax
import jax.numpy as jnp
from jax import lax
from jax.experimental import pallas as pl
from jax.experimental.pallas import tpu as pltpu
from jax.sharding import PartitionSpec as P


DH,BS,TAB=32,128,16
G=4
SCALE=DH**-0.5
LOG2E=math.log2(math.e)
F32=jnp.float32
BF=jnp.bfloat16
NT=(((1,),(1,)),((),()))
NN=(((1,),(0,)),((),()))


def dot(a,b,dims): return lax.dot_general(a,b,dims,preferred_element_type=F32)


def loop2(pairs,f):
    def two(k,c):
        f(2*k,0); f(2*k+1,0)
        return c
    lax.fori_loop(0,pairs//2,two,0)
    @pl.when(pairs%2==1)
    def _(): f(pairs-1,0)


def attend_kernel(first, *refs):
    idx,cnt,chk,q,gate,cot,bias=refs[:7]
    pieces=refs[7:15]
    k=15
    prev=None
    if not first: prev=refs[15:19]; k=19
    dq,gg,bg=refs[k:k+3]
    terms=refs[k+3:k+7]
    s_ref,e_ref,m_ref,l_ref,o_ref,off_ref,qm,qt,dom,domt,acc,kv,sem=refs[k+7:]
    for m in range(8):
        pltpu.make_async_copy(pieces[m],kv.at[pl.ds(4*m,4)],sem.at[m]).start()
    lane=lax.broadcasted_iota(jnp.int32,(BS,BS),1)//DH
    acc[...]=jnp.zeros(acc.shape,F32)
    for m in range(8):
        pltpu.make_async_copy(pieces[m],kv.at[pl.ds(4*m,4)],sem.at[m]).wait()
    def block(j,carry):
        n=cnt[j]
        pairs=(n+1)//2
        qj=q[j]
        for g in range(G):
            r=slice(g*BS,(g+1)*BS)
            v=jnp.where(lane==g,qj,jnp.zeros_like(qj))
            qm[r,:]=v
            qt[:,r]=v.T
        m_ref[...]=jnp.full(m_ref.shape,-jnp.inf,F32)
        l_ref[...]=jnp.zeros(l_ref.shape,F32)
        o_ref[...]=jnp.zeros(o_ref.shape,F32)
        def both(p,w):
            return jnp.concatenate([kv[idx[j,2*p],w],kv[idx[j,2*p+1],w]],0)
        def score(p,c):
            k2=both(p,0)
            S=dot(qm[...],k2,NT)*(SCALE*LOG2E)
            for h in range(2):
                b0=bias[j,h,2*p].astype(F32)*LOG2E
                b1=bias[j,h,2*p+1].astype(F32)*LOG2E
                b1=jnp.where(2*p+1<n,b1,-1e30)
                for i in range(2):
                    g=2*i+h
                    r=slice(g*BS,(g+1)*BS)
                    s=S[r,:]
                    s0=s[:,:BS]+b0; s1=s[:,BS:]+b1
                    s_ref[p,r,:BS]=s0
                    s_ref[p,r,BS:]=s1
                    m_ref[r,:]=jnp.maximum(m_ref[r,:],jnp.maximum(s0,s1))
            return c
        loop2(pairs,score)
        m_ref[...]=jnp.broadcast_to(jnp.max(m_ref[...],axis=1,keepdims=True),m_ref.shape)
        def attend(p,c):
            v2=both(p,1)
            for g in range(G):
                r=slice(g*BS,(g+1)*BS)
                m=m_ref[r,:]
                e0=jnp.exp2(s_ref[p,r,:BS]-m); e1=jnp.exp2(s_ref[p,r,BS:]-m)
                l_ref[r,:]+=e0+e1
                e=jnp.concatenate([e0.astype(BF),e1.astype(BF)],1)
                e_ref[p,r,:]=e
            o_ref[...]+=dot(e_ref[p],v2,NN)
            return c
        loop2(pairs,attend)
        att=jnp.zeros((BS,BS),F32); inv=[]
        for g in range(G):
            r=slice(g*BS,(g+1)*BS)
            inv.append(1.0/jnp.sum(l_ref[r,:],axis=1,keepdims=True))
            att=jnp.where(lane==g,o_ref[r,:]*inv[g],att)
        c=cot[j].astype(F32)
        opened=1.0/(1.0+jnp.exp(-gate[j].astype(F32)))
        gg[j]=(c*att*opened*(1.0-opened)).astype(BF)
        core=(c*opened).astype(BF).astype(F32)
        for g in range(G):
            r=slice(g*BS,(g+1)*BS)
            d=jnp.where(lane==g,core*inv[g],0.0).astype(BF)
            dom[r,:]=d
            domt[:,r]=d.T
            off_ref[r,:]=jnp.broadcast_to(jnp.sum(d.astype(F32)*att,axis=1,keepdims=True),(BS,BS))
        o_ref[...]=jnp.zeros(o_ref.shape,F32)
        def backward(p,c):
            a0=idx[j,2*p]; a1=idx[j,2*p+1]
            ch=chk[p]
            k2=both(p,0); v2=both(p,1)
            halves=[]; total=[None,None]
            WG=dot(dom[...],v2,NT)
            for g in range(G):
                r=slice(g*BS,(g+1)*BS); h=g%2
                off=off_ref[r,:]
                wg=WG[r,:]
                ds=e_ref[p,r,:].astype(F32)*(wg-jnp.concatenate([off,off],1))
                if g<2: total[h]=ds
                else:
                    b=(total[h]+ds).astype(BF)
                    bg[ch,j,h,0]=b[:,:BS]; bg[ch,j,h,1]=b[:,BS:]
                half=ds.astype(BF)
                halves.append(half)
            hs=jnp.concatenate(halves,0)
            o_ref[...]+=dot(hs,k2,NN)
            dk=dot(qt[...],hs,NN)
            dv=dot(domt[...],e_ref[p],NN)
            acc[a0,0]+=dk[:,:BS]; acc[a1,0]+=dk[:,BS:]
            acc[a0,1]+=dv[:,:BS]; acc[a1,1]+=dv[:,BS:]
            return c
        loop2(pairs,backward)
        def clear(p,c):
            z=jnp.zeros((2,2,BS,BS),BF)
            bg[chk[p],j]=z
            return c
        lax.fori_loop(pairs,8,clear,0)
        x=jnp.zeros((BS,BS),F32)
        for g in range(G):
            x=jnp.where(lane==g,o_ref[g*BS:(g+1)*BS,:],x)
        dq[j]=(x*SCALE).astype(BF)
        return carry
    lax.fori_loop(0,2,block,0)
    for dy in range(4):
        def store(b,c):
            a=acc[8*dy+b]
            if not first: a=a+prev[dy][b].astype(F32)
            terms[dy][b]=a.astype(BF)
            return c
        lax.fori_loop(0,8,store,0)


def attend_blocks(idx,cnt,chk,q,gate,cot,bias,pieces,prev):
    first=prev is None
    SM=pl.BlockSpec(memory_space=pltpu.SMEM)
    VM=pl.BlockSpec(memory_space=pltpu.VMEM)
    AN=pl.BlockSpec(memory_space=pl.ANY)
    args=[idx,cnt,chk,q,gate,cot,bias,*pieces]
    specs=[SM]*3+[VM]*4+[AN]*8
    if not first:
        args+=prev
        specs+=[VM]*4

    def kernel(*refs):
        attend_kernel(first,*refs)

    shapes=((2,BS,BS),(2,BS,BS),(8,2,2,2,BS,BS))+((8,2,BS,BS),)*4
    return pl.pallas_call(
        kernel,
        out_shape=tuple(jax.ShapeDtypeStruct(s,BF) for s in shapes),
        in_specs=specs,
        out_specs=(VM,)*7,
        scratch_shapes=[pltpu.VMEM((8,G*BS,2*BS),F32),pltpu.VMEM((8,G*BS,2*BS),BF)]
        +[pltpu.VMEM((G*BS,BS),F32)]*4
        +[pltpu.VMEM((G*BS,BS),BF),pltpu.VMEM((BS,G*BS),BF)]*2
        +[pltpu.VMEM((32,2,BS,BS),F32),pltpu.VMEM((32,2,BS,BS),BF),pltpu.SemaphoreType.DMA((8,))],
        compiler_params=pltpu.CompilerParams(vmem_limit_bytes=20<<20),
        cost_estimate=pl.CostEstimate(flops=10_000_000_000,bytes_accessed=24<<20,transcendentals=4<<20),
        name="attend_blocks",
    )(*args)


def join_kernel(p,xs,cs,xc,sel,k_out,v_out):
    for w,out in ((0,k_out),(1,v_out)):
        for b in range(2):
            own=p[b,w].astype(F32)+xs[b,w].astype(F32)
            far=cs[b,w].astype(F32)+xc[b,w].astype(F32)
            if w==0:
                own=own*SCALE
                far=far*SCALE
            both=jnp.concatenate([own.astype(BF).T,far.astype(BF).T],1)
            full=dot(both,sel[...],NT).astype(BF)
            out[0,b*BS:(b+1)*BS,:]=full[:,:BS]
            out[1,b*BS:(b+1)*BS,:]=full[:,BS:]


def unite_kernel(q,g,back,sel,q_out,g_out):
    for w,mine,out in ((0,q,q_out),(1,g,g_out)):
        for b in range(2):
            both=jnp.concatenate([mine[b],back[w,b]],1)
            full=dot(both,sel[...],NT).astype(BF)
            out[0,b*BS:(b+1)*BS,:]=full[:,:BS]
            out[1,b*BS:(b+1)*BS,:]=full[:,BS:]


def small_call(kernel,*args):
    VM=pl.BlockSpec(memory_space=pltpu.VMEM)
    return pl.pallas_call(
        kernel,
        out_shape=(jax.ShapeDtypeStruct((2,2*BS,BS),BF),)*2,
        in_specs=[VM]*len(args),
        out_specs=(VM,)*2,
        compiler_params=pltpu.CompilerParams(vmem_limit_bytes=8<<20),
        cost_estimate=pl.CostEstimate(flops=1<<28,bytes_accessed=1<<20,transcendentals=0),
    )(*args)


def to_col(x,dy,dx,dc):
    pairs=[]
    for s in range(16):
        sy,sx,sc=s//4,(s//2)%2,s%2
        pairs.append((s,((sy+dy)%4)*4+(sx^dx)*2+(sc^dc)))
    return lax.ppermute(x,"col",pairs)


def to_row(x,dx,dz):
    pairs=[(s,((s//4)^dx)*4+(s%4+dz)%4) for s in range(8)]
    return lax.ppermute(x,"row",pairs)


def swap(x):
    return to_col(x,0,0,1)


def plus(*terms):
    total=terms[0].astype(F32)
    for t in terms[1:]:
        total=total+t.astype(F32)
    return total


def body(
    query_vectors,
    key_vectors,
    value_vectors,
    gate_logits,
    cotangent,
    pair_bias,
    block_table,
    valid_counts,
):
    col=lax.axis_index("col")
    row=lax.axis_index("row")
    y,xl,core=col//4,(col//2)%2,col%2
    xh,z=row//4,row%4

    src=lax.broadcasted_iota(jnp.int32,(256,256),0)
    dst=lax.broadcasted_iota(jnp.int32,(256,256),1)
    want=((dst%BS)//64)*BS+((dst//BS)^core)*64+dst%64
    sel=lax.optimization_barrier((src==want).astype(BF))

    def split(x):
        both=lax.dot_general(x.reshape(2*BS,2*BS),sel,NN,preferred_element_type=F32).astype(BF)
        return both[:,:BS].reshape(2,BS,BS),both[:,BS:].reshape(2,BS,BS)

    k_mine,k_send=split(key_vectors)
    v_mine,v_send=split(value_vectors)
    shard=jnp.concatenate([jnp.stack([k_mine,v_mine],1),swap(jnp.stack([k_send,v_send],1))],0)
    shard,pair_bias=lax.optimization_barrier((shard,pair_bias))
    pieces=[]
    for dy in range(4):
        for dx in range(2):
            pieces.append(to_col(shard,(4-dy)%4,dx,0) if dy+dx else shard)

    table=jnp.concatenate([block_table,valid_counts[:,None]],1)
    tables=[table,swap(table)]

    def places(t):
        ids=t[:,:TAB]
        owner=ids//2
        chip=((owner//4-y)%4)*2+(((owner//2)%2)^xl)
        return chip*4+((owner%2)^core)*2+ids%2

    dest=jnp.arange(8,dtype=jnp.int32)
    far=(dest//4)^xh
    turn=(dest%4-z)%4

    bias=pair_bias.transpose(0,1,3,2,4)
    bias_mine=lax.dynamic_slice_in_dim(bias,2*core,2,1)
    bias_other=swap(lax.dynamic_slice_in_dim(bias,2-2*core,2,1))
    parts=[split(x) for x in (query_vectors,gate_logits,cotangent)]
    mine=[p[0] for p in parts]
    other=swap(jnp.stack([p[1] for p in parts],0))

    ready=(places(tables[0]),tables[0][:,TAB],places(tables[1]),tables[1][:,TAB],mine,other,bias_mine,bias_other,pieces)
    idx0,cnt0,idx1,cnt1,mine,other,bias_mine,bias_other,pieces=lax.optimization_barrier(ready)
    dq0,gg0,bg0,*terms=attend_blocks(idx0,cnt0,turn*2+far,*mine,bias_mine,pieces,None)
    bg0=bg0.reshape(4,2,2,2,2,BS,BS)
    bg0_in=[]
    for dz in range(1,4):
        bg0_in.append(to_row(bg0[dz],0,dz))
    dq1,gg1,bg1,*terms=attend_blocks(
        idx1,cnt1,far*4+turn,other[0],other[1],other[2],bias_other,pieces,terms
    )
    bg1=bg1.reshape(2,4,2,2,2,BS,BS)

    terms=[t.reshape(2,4,2,BS,BS) for t in terms]
    part=plus(terms[0],*[to_col(terms[dy],dy,0,0) for dy in range(1,4)]).astype(BF)
    bg1=plus(bg1[0],to_row(bg1[1],1,0)).astype(BF)
    bg0=plus(bg0[0],*bg0_in).astype(BF)
    bias1_in=[to_row(bg1[dz],0,dz) for dz in range(1,4)]
    bias0=plus(bg0[0],to_row(bg0[1],1,0)).astype(BF)
    bias1=plus(bg1[0],*bias1_in).astype(BF)
    bias_back=swap(bias1)

    q_back=swap(jnp.stack([dq1,gg1],0))
    query_grad,gate_grad=small_call(unite_kernel,dq0,gg0,q_back,sel)
    key_grad,value_grad=small_call(
        join_kernel,
        part[0,:2],
        to_col(part[1,:2],0,1,0),
        swap(part[0,2:]),
        to_col(part[1,2:],0,1,1),
        sel,
    )

    a=jnp.where(core==0,bias0,bias_back)
    b=jnp.where(core==0,bias_back,bias0)
    bias_grad=jnp.concatenate([a,b],1).transpose(0,1,3,2,4)

    def rows(x):
        return x.transpose(1,0,2)

    return rows(query_grad),rows(key_grad),rows(value_grad),rows(gate_grad),bias_grad


def solution(mesh):
    return jax.shard_map(
        body,
        mesh=mesh,
        in_specs=(
            P("col","row",None),
            P("col","row",None),
            P("col","row",None),
            P("col","row",None),
            P("col","row",None),
            P("col",None,None,None,None),
            P("col",None),
            P("col"),
        ),
        out_specs=(
            P("col","row",None),
            P("col","row",None),
            P("col","row",None),
            P("col","row",None),
            P("col",None,None,"row",None),
        ),
        check_vma=False,
    )
```

```python
import math

import jax
import jax.numpy as jnp
from jax import lax
from jax.experimental import pallas as pl
from jax.experimental.pallas import tpu as pltpu
from jax.sharding import PartitionSpec as P


DH,BS,TAB=32,128,16
G=4
SCALE=DH**-0.5
LOG2E=math.log2(math.e)
F32=jnp.float32
BF=jnp.bfloat16
NT=(((1,),(1,)),((),()))
NN=(((1,),(0,)),((),()))


def dot(a,b,dims): return lax.dot_general(a,b,dims,preferred_element_type=F32)


def loop2(pairs,f):
    def two(k,c):
        f(2*k,0); f(2*k+1,0)
        return c

    lax.fori_loop(0,pairs//2,two,0)

    @pl.when(pairs%2==1)
    def _(): f(pairs-1,0)


def attend_kernel(first,*refs):
    idx,cnt,chk,q,gate,cot,bias=refs[:7]
    pieces=refs[7:15]
    if first:
        dq,gg,bg,acc=refs[15:19]
        rest=refs[19:]
    else:
        dq,gg,bg,acc=refs[16:20]
        terms=refs[20:28]
        rest=refs[28:]
    s_ref,e_ref,m_ref,l_ref,o_ref,off_ref,qm,qt,dom,domt,kv,sem=rest
    for m in range(8):
        pltpu.make_async_copy(pieces[m],kv.at[pl.ds(4*m,4)],sem.at[m]).start()
    lane=lax.broadcasted_iota(jnp.int32,(BS,BS),1)//DH
    chan=lax.broadcasted_iota(jnp.int32,(BS,BS),0)//DH
    if first:
        acc[...]=jnp.zeros(acc.shape,F32)
    for m in range(8):
        pltpu.make_async_copy(pieces[m],kv.at[pl.ds(4*m,4)],sem.at[m]).wait()

    def block(j,carry):
        n=cnt[j]
        pairs=(n+1)//2
        qj=q[j]
        qj_t=qj.T
        for g in range(G):
            r=slice(g*BS,(g+1)*BS)
            qm[r,:]=jnp.where(lane==g,qj,jnp.zeros_like(qj))
            qt[:,r]=jnp.where(chan==g,qj_t,jnp.zeros_like(qj_t))
        m_ref[...]=jnp.full(m_ref.shape,-jnp.inf,F32)
        l_ref[...]=jnp.zeros(l_ref.shape,F32)
        o_ref[...]=jnp.zeros(o_ref.shape,F32)

        def both(p,w):
            return jnp.concatenate([kv[idx[j,2*p],w],kv[idx[j,2*p+1],w]],0)

        def score(p,c):
            k2=both(p,0)
            S=dot(qm[...],k2,NT)*(SCALE*LOG2E)
            for h in range(2):
                b0=bias[j,h,2*p].astype(F32)*LOG2E
                b1=bias[j,h,2*p+1].astype(F32)*LOG2E
                b1=jnp.where(2*p+1<n,b1,-1e30)
                for i in range(2):
                    g=2*i+h
                    r=slice(g*BS,(g+1)*BS)
                    s=S[r,:]
                    s0=s[:,:BS]+b0; s1=s[:,BS:]+b1
                    s_ref[p,r,:BS]=s0
                    s_ref[p,r,BS:]=s1
                    m_ref[r,:]=jnp.maximum(m_ref[r,:],jnp.maximum(s0,s1))
            return c

        loop2(pairs,score)
        m_ref[...]=jnp.broadcast_to(jnp.max(m_ref[...],axis=1,keepdims=True),m_ref.shape)

        def attend(p,c):
            v2=both(p,1)
            for g in range(G):
                r=slice(g*BS,(g+1)*BS)
                m=m_ref[r,:]
                e0=jnp.exp2(s_ref[p,r,:BS]-m); e1=jnp.exp2(s_ref[p,r,BS:]-m)
                l_ref[r,:]+=e0+e1
                e=jnp.concatenate([e0.astype(BF),e1.astype(BF)],1)
                e_ref[p,r,:]=e
            o_ref[...]+=dot(e_ref[p],v2,NN)
            return c

        loop2(pairs,attend)
        att=jnp.zeros((BS,BS),F32)
        inv=jnp.zeros((BS,BS),F32)
        for g in range(G):
            r=slice(g*BS,(g+1)*BS)
            one=1.0/jnp.sum(l_ref[r,:],axis=1,keepdims=True)
            att=jnp.where(lane==g,o_ref[r,:],att)
            inv=jnp.where(lane==g,one,inv)
        att=att*inv
        c=cot[j].astype(F32)
        opened=1.0/(1.0+jnp.exp(-gate[j].astype(F32)))
        gg[j]=(c*att*opened*(1.0-opened)).astype(BF)
        d=((c*opened).astype(BF).astype(F32)*inv).astype(BF)
        d_t=d.T
        x=d.astype(F32)*att
        for g in range(G):
            r=slice(g*BS,(g+1)*BS)
            dom[r,:]=jnp.where(lane==g,d,jnp.zeros_like(d))
            domt[:,r]=jnp.where(chan==g,d_t,jnp.zeros_like(d_t))
            off=jnp.sum(jnp.where(lane==g,x,0.0),axis=1,keepdims=True)
            off_ref[r,:]=jnp.broadcast_to(off,(BS,BS))
        o_ref[...]=jnp.zeros(o_ref.shape,F32)

        def backward(p,c):
            a0=idx[j,2*p]; a1=idx[j,2*p+1]
            ch=chk[p]
            k2=both(p,0); v2=both(p,1)
            halves=[]; total=[None,None]
            WG=dot(dom[...],v2,NT)
            for g in range(G):
                r=slice(g*BS,(g+1)*BS); h=g%2
                off=off_ref[r,:]
                wg=WG[r,:]
                ds=e_ref[p,r,:].astype(F32)*(wg-jnp.concatenate([off,off],1))
                if g<2: total[h]=ds
                else:
                    b=(total[h]+ds).astype(BF)
                    bg[ch,j,h,0]=b[:,:BS]; bg[ch,j,h,1]=b[:,BS:]
                half=ds.astype(BF)
                halves.append(half)
            hs=jnp.concatenate(halves,0)
            o_ref[...]+=dot(hs,k2,NN)
            dk=dot(qt[...],hs,NN)
            dv=dot(domt[...],e_ref[p],NN)
            acc[a0,0]+=dk[:,:BS]; acc[a1,0]+=dk[:,BS:]
            acc[a0,1]+=dv[:,:BS]; acc[a1,1]+=dv[:,BS:]
            return c

        loop2(pairs,backward)

        def clear(p,c):
            z=jnp.zeros((2,2,BS,BS),BF)
            bg[chk[p],j]=z
            return c

        lax.fori_loop(pairs,8,clear,0)
        x=jnp.zeros((BS,BS),F32)
        for g in range(G):
            x=jnp.where(lane==g,o_ref[g*BS:(g+1)*BS,:],x)
        dq[j]=(x*SCALE).astype(BF)
        return carry

    lax.fori_loop(0,2,block,0)
    if not first:
        for m in range(8):
            terms[m][...]=acc[4*m:4*m+4].astype(BF)


def attend_blocks(idx,cnt,chk,q,gate,cot,bias,pieces,prev):
    first=prev is None
    SM=pl.BlockSpec(memory_space=pltpu.SMEM)
    VM=pl.BlockSpec(memory_space=pltpu.VMEM)
    AN=pl.BlockSpec(memory_space=pl.ANY)
    args=[idx,cnt,chk,q,gate,cot,bias,*pieces]
    specs=[SM]*3+[VM]*4+[AN]*8
    shapes=[((2,BS,BS),BF),((2,BS,BS),BF),((8,2,2,2,BS,BS),BF),((32,2,BS,BS),F32)]
    if not first:
        args.append(prev)
        specs.append(VM)
        shapes+=[((4,2,BS,BS),BF)]*8

    def kernel(*refs):
        attend_kernel(first,*refs)

    return pl.pallas_call(
        kernel,
        out_shape=tuple(jax.ShapeDtypeStruct(*s) for s in shapes),
        in_specs=specs,
        out_specs=(VM,)*len(shapes),
        scratch_shapes=[pltpu.VMEM((8,G*BS,2*BS),F32),pltpu.VMEM((8,G*BS,2*BS),BF)]
        +[pltpu.VMEM((G*BS,BS),F32)]*4
        +[pltpu.VMEM((G*BS,BS),BF),pltpu.VMEM((BS,G*BS),BF)]*2
        +[pltpu.VMEM((32,2,BS,BS),BF),pltpu.SemaphoreType.DMA((8,))],
        input_output_aliases={} if first else {15:3},
        compiler_params=pltpu.CompilerParams(vmem_limit_bytes=20<<20),
        cost_estimate=pl.CostEstimate(flops=10_000_000_000,bytes_accessed=24<<20,transcendentals=4<<20),
        name="attend_blocks",
    )(*args)


def join_kernel(own,far,sel,k_out,v_out):
    for w,out in ((0,k_out),(1,v_out)):
        for b in range(2):
            both=jnp.concatenate([own[b,w].T,far[b,w].T],1)
            full=dot(both,sel[...],NT).astype(BF)
            out[0,b*BS:(b+1)*BS,:]=full[:,:BS]
            out[1,b*BS:(b+1)*BS,:]=full[:,BS:]


def unite_kernel(q,g,back,sel,q_out,g_out):
    for w,mine,out in ((0,q,q_out),(1,g,g_out)):
        for b in range(2):
            both=jnp.concatenate([mine[b],back[w,b]],1)
            full=dot(both,sel[...],NT).astype(BF)
            out[0,b*BS:(b+1)*BS,:]=full[:,:BS]
            out[1,b*BS:(b+1)*BS,:]=full[:,BS:]


def small_call(kernel,*args):
    VM=pl.BlockSpec(memory_space=pltpu.VMEM)
    return pl.pallas_call(
        kernel,
        out_shape=(jax.ShapeDtypeStruct((2,2*BS,BS),BF),)*2,
        in_specs=[VM]*len(args),
        out_specs=(VM,)*2,
        compiler_params=pltpu.CompilerParams(vmem_limit_bytes=8<<20),
        cost_estimate=pl.CostEstimate(flops=1<<28,bytes_accessed=1<<20,transcendentals=0),
    )(*args)


def to_col(x,dy,dx,dc):
    pairs=[]
    for s in range(16):
        sy,sx,sc=s//4,(s//2)%2,s%2
        pairs.append((s,((sy+dy)%4)*4+(sx^dx)*2+(sc^dc)))
    return lax.ppermute(x,"col",pairs)


def to_row(x,dx,dz):
    pairs=[(s,((s//4)^dx)*4+(s%4+dz)%4) for s in range(8)]
    return lax.ppermute(x,"row",pairs)


def cross(x):
    pairs=[]
    for r in range(8):
        for c in range(16):
            pairs.append((r*16+c,(r^4)*16+(c^1)))
    return lax.ppermute(x,("row","col"),pairs)


def swap(x):
    return to_col(x,0,0,1)


def plus(*terms):
    total=terms[0].astype(F32)
    for t in terms[1:]:
        total=total+t.astype(F32)
    return total


def body(
    query_vectors,
    key_vectors,
    value_vectors,
    gate_logits,
    cotangent,
    pair_bias,
    block_table,
    valid_counts,
):
    col=lax.axis_index("col")
    row=lax.axis_index("row")
    y,xl,core=col//4,(col//2)%2,col%2
    xh,z=row//4,row%4

    src=lax.broadcasted_iota(jnp.int32,(256,256),0)
    dst=lax.broadcasted_iota(jnp.int32,(256,256),1)
    want=((dst%BS)//64)*BS+((dst//BS)^core)*64+dst%64
    sel=lax.optimization_barrier((src==want).astype(BF))

    def split(x):
        both=lax.dot_general(x.reshape(2*BS,2*BS),sel,NN,preferred_element_type=F32).astype(BF)
        return both[:,:BS].reshape(2,BS,BS),both[:,BS:].reshape(2,BS,BS)

    k_mine,k_send=split(key_vectors)
    v_mine,v_send=split(value_vectors)
    shard=jnp.concatenate([jnp.stack([k_mine,v_mine],1),swap(jnp.stack([k_send,v_send],1))],0)
    shard,pair_bias=lax.optimization_barrier((shard,pair_bias))

    def gather(x,dy,dx):
        return to_col(x,(4-dy)%4,dx,0)

    near=gather(shard,0,1)
    up,down,across=gather(shard,1,0),gather(shard,3,0),gather(shard,2,0)
    pieces=[shard, near, up, gather(near,1,0), across, gather(across,0,1), down, gather(near,3,0)]

    table=jnp.concatenate([block_table,valid_counts[:,None]],1)
    tables=[table,swap(table)]

    def places(t):
        ids=t[:,:TAB]
        owner=ids//2
        chip=((owner//4-y)%4)*2+(((owner//2)%2)^xl)
        return chip*4+((owner%2)^core)*2+ids%2

    dest=jnp.arange(8,dtype=jnp.int32)
    far=(dest//4)^xh
    turn=(dest%4-z)%4

    bias=pair_bias.transpose(0,1,3,2,4)
    bias_mine=lax.dynamic_slice_in_dim(bias,2*core,2,1)
    bias_other=swap(lax.dynamic_slice_in_dim(bias,2-2*core,2,1))
    parts=[split(x) for x in (query_vectors,gate_logits,cotangent)]
    mine=[p[0] for p in parts]
    other=swap(jnp.stack([p[1] for p in parts],0))

    ready=(places(tables[0]),tables[0][:,TAB],places(tables[1]),tables[1][:,TAB],mine,other,bias_mine,bias_other,pieces)
    idx0,cnt0,idx1,cnt1,mine,other,bias_mine,bias_other,pieces=lax.optimization_barrier(ready)
    dq0,gg0,bg0,acc=attend_blocks(idx0,cnt0,turn*2+far,*mine,bias_mine,pieces,None)
    bg0=bg0.reshape(4,2,2,2,2,BS,BS)

    def row_sums(x):
        out=[x[0]]
        for dz in range(1,4):
            out.append(to_row(x[dz],0,dz))
        return out

    bg0=row_sums(bg0)
    dq1,gg1,bg1,_,*t=attend_blocks(
        idx1,cnt1,turn*2+far,other[0],other[1],other[2],bias_other,pieces,acc
    )
    bg1=bg1.reshape(4,2,2,2,2,BS,BS)

    def step(x,dy,dx):
        return to_col(x,dy,dx,0)

    from_down,from_up=step(t[3],1,0),step(t[7],3,0)
    from_near=step(t[5],0,1)
    bg1=row_sums(bg1)
    steps=[step(t[2],1,0),step(t[6],3,0)]
    bg0=plus(*bg0).astype(BF)
    bg0_far=to_row(bg0[1],1,0)
    steps.append(step(plus(t[1],from_down,from_up).astype(BF),0,1))
    steps.append(step(plus(t[4],from_near).astype(BF),2,0))
    q_back=swap(jnp.stack([dq1,gg1],0))
    query_grad,gate_grad=small_call(unite_kernel,dq0,gg0,q_back,sel)
    bias0=plus(bg0[0],bg0_far).astype(BF)
    own=plus(t[0],*steps)
    own=jnp.stack([own[:,0]*SCALE,own[:,1]],1).astype(BF)
    own_far=swap(own[2:])
    key_grad,value_grad=small_call(join_kernel,own[:2],own_far,sel)

    bg1=plus(*bg1).astype(BF)
    turned=cross(bg1[1])
    bias1=plus(swap(bg1[0]),turned).astype(BF)

    a=jnp.where(core==0,bias0,bias1)
    b=jnp.where(core==0,bias1,bias0)
    bias_grad=jnp.concatenate([a,b],1).transpose(0,1,3,2,4)

    def rows(x):
        return x.transpose(1,0,2)

    return rows(query_grad),rows(key_grad),rows(value_grad),rows(gate_grad),bias_grad


def solution(mesh):
    return jax.shard_map(
        body,
        mesh=mesh,
        in_specs=(
            P("col","row",None),
            P("col","row",None),
            P("col","row",None),
            P("col","row",None),
            P("col","row",None),
            P("col",None,None,None,None),
            P("col",None),
            P("col"),
        ),
        out_specs=(
            P("col","row",None),
            P("col","row",None),
            P("col","row",None),
            P("col","row",None),
            P("col",None,None,"row",None),
        ),
        check_vma=False,
    )
```

```python
import math

import jax
import jax.numpy as jnp
from jax import lax
from jax.experimental import pallas as pl
from jax.experimental.pallas import tpu as pltpu
from jax.sharding import PartitionSpec as P


DH,BS,TAB=32,128,16
G=4
SCALE=DH**-0.5
LOG2E=math.log2(math.e)
F32=jnp.float32
BF=jnp.bfloat16
NT=(((1,),(1,)),((),()))
NN=(((1,),(0,)),((),()))


def dot(a,b,dims): return lax.dot_general(a,b,dims,preferred_element_type=F32)


def loop2(pairs,f):
    def two(k,c):
        f(2*k,0); f(2*k+1,0)
        return c

    lax.fori_loop(0,pairs//2,two,0)

    @pl.when(pairs%2==1)
    def _(): f(pairs-1,0)


def attend_kernel(first,*refs):
    idx,cnt,chk,qgc,bias=refs[:5]
    q,gate,cot=qgc.at[0],qgc.at[1],qgc.at[2]
    pieces=refs[5:13]
    if first:
        dq,gg,bg,acc=refs[13:17]
        rest=refs[17:]
    else:
        dq,gg,bg,acc=refs[14:18]
        terms=refs[18:26]
        rest=refs[26:]
    s_ref,e_ref,m_ref,l_ref,o_ref,off_ref,qm,qt,dom,domt,kv,sem=rest
    for m in range(8):
        pltpu.make_async_copy(pieces[m],kv.at[pl.ds(4*m,4)],sem.at[m]).start()
    lane=lax.broadcasted_iota(jnp.int32,(BS,BS),1)//DH
    chan=lax.broadcasted_iota(jnp.int32,(BS,BS),0)//DH
    if first:
        acc[...]=jnp.zeros(acc.shape,F32)
    for m in range(8):
        pltpu.make_async_copy(pieces[m],kv.at[pl.ds(4*m,4)],sem.at[m]).wait()

    def block(j,carry):
        n=cnt[j]
        pairs=(n+1)//2
        qj=q[j]
        qj_t=qj.T
        for g in range(G):
            r=slice(g*BS,(g+1)*BS)
            qm[r,:]=jnp.where(lane==g,qj,jnp.zeros_like(qj))
            qt[:,r]=jnp.where(chan==g,qj_t,jnp.zeros_like(qj_t))
        m_ref[...]=jnp.full(m_ref.shape,-jnp.inf,F32)
        l_ref[...]=jnp.zeros(l_ref.shape,F32)
        o_ref[...]=jnp.zeros(o_ref.shape,F32)

        def both(p,w):
            return jnp.concatenate([kv[idx[j,2*p],w],kv[idx[j,2*p+1],w]],0)

        def score(p,c):
            k2=both(p,0)
            S=dot(qm[...],k2,NT)*(SCALE*LOG2E)
            for h in range(2):
                b0=bias[j,h,2*p].astype(F32)*LOG2E
                b1=bias[j,h,2*p+1].astype(F32)*LOG2E
                b1=jnp.where(2*p+1<n,b1,-1e30)
                for i in range(2):
                    g=2*i+h
                    r=slice(g*BS,(g+1)*BS)
                    s=S[r,:]
                    s0=s[:,:BS]+b0; s1=s[:,BS:]+b1
                    s_ref[p,r,:BS]=s0
                    s_ref[p,r,BS:]=s1
                    m_ref[r,:]=jnp.maximum(m_ref[r,:],jnp.maximum(s0,s1))
            return c

        loop2(pairs,score)
        m_ref[...]=jnp.broadcast_to(jnp.max(m_ref[...],axis=1,keepdims=True),m_ref.shape)

        def attend(p,c):
            v2=both(p,1)
            for g in range(G):
                r=slice(g*BS,(g+1)*BS)
                m=m_ref[r,:]
                e0=jnp.exp2(s_ref[p,r,:BS]-m); e1=jnp.exp2(s_ref[p,r,BS:]-m)
                l_ref[r,:]+=e0+e1
                e=jnp.concatenate([e0.astype(BF),e1.astype(BF)],1)
                e_ref[p,r,:]=e
            o_ref[...]+=dot(e_ref[p],v2,NN)
            return c

        loop2(pairs,attend)
        att=jnp.zeros((BS,BS),F32)
        inv=jnp.zeros((BS,BS),F32)
        for g in range(G):
            r=slice(g*BS,(g+1)*BS)
            one=1.0/jnp.sum(l_ref[r,:],axis=1,keepdims=True)
            att=jnp.where(lane==g,o_ref[r,:],att)
            inv=jnp.where(lane==g,one,inv)
        att=att*inv
        c=cot[j].astype(F32)
        opened=1.0/(1.0+jnp.exp(-gate[j].astype(F32)))
        gg[j]=(c*att*opened*(1.0-opened)).astype(BF)
        d=((c*opened).astype(BF).astype(F32)*inv).astype(BF)
        d_t=d.T
        x=d.astype(F32)*att
        for g in range(G):
            r=slice(g*BS,(g+1)*BS)
            dom[r,:]=jnp.where(lane==g,d,jnp.zeros_like(d))
            domt[:,r]=jnp.where(chan==g,d_t,jnp.zeros_like(d_t))
            off=jnp.sum(jnp.where(lane==g,x,0.0),axis=1,keepdims=True)
            off_ref[r,:]=jnp.broadcast_to(off,(BS,BS))
        o_ref[...]=jnp.zeros(o_ref.shape,F32)

        def backward(p,c):
            a0=idx[j,2*p]; a1=idx[j,2*p+1]
            out=bg.at[chk[0,p],j] if first else bg.at[j,chk[j,p]]
            k2=both(p,0); v2=both(p,1)
            halves=[]; total=[None,None]
            WG=dot(dom[...],v2,NT)
            for g in range(G):
                r=slice(g*BS,(g+1)*BS); h=g%2
                off=off_ref[r,:]
                wg=WG[r,:]
                ds=e_ref[p,r,:].astype(F32)*(wg-jnp.concatenate([off,off],1))
                if g<2: total[h]=ds
                else:
                    b=(total[h]+ds).astype(BF)
                    out[h,0]=b[:,:BS]; out[h,1]=b[:,BS:]
                half=ds.astype(BF)
                halves.append(half)
            hs=jnp.concatenate(halves,0)
            o_ref[...]+=dot(hs,k2,NN)
            dk=dot(qt[...],hs,NN)
            dv=dot(domt[...],e_ref[p],NN)
            acc[a0,0]+=dk[:,:BS]; acc[a1,0]+=dk[:,BS:]
            acc[a0,1]+=dv[:,:BS]; acc[a1,1]+=dv[:,BS:]
            return c

        loop2(pairs,backward)

        def clear(p,c):
            out=bg.at[chk[0,p],j] if first else bg.at[j,chk[j,p]]
            out[...]=jnp.zeros((2,2,BS,BS),BF)
            return c

        lax.fori_loop(pairs,8,clear,0)
        x=jnp.zeros((BS,BS),F32)
        for g in range(G):
            x=jnp.where(lane==g,o_ref[g*BS:(g+1)*BS,:],x)
        dq[j]=(x*SCALE).astype(BF)
        return carry

    lax.fori_loop(0,2,block,0)
    if not first:
        for m in range(8):
            terms[m][...]=acc[4*m:4*m+4].astype(BF)


def attend_blocks(idx,cnt,chk,qgc,bias,pieces,prev):
    first=prev is None
    SM=pl.BlockSpec(memory_space=pltpu.SMEM)
    VM=pl.BlockSpec(memory_space=pltpu.VMEM)
    AN=pl.BlockSpec(memory_space=pl.ANY)
    args=[idx,cnt,chk,qgc,bias,*pieces]
    specs=[SM]*3+[VM]*2+[AN]*8
    lead=(8,2) if first else (2,8)
    shapes=[((2,BS,BS),BF),((2,BS,BS),BF),(lead+(2,2,BS,BS),BF),((32,2,BS,BS),F32)]
    if not first:
        args.append(prev)
        specs.append(VM)
        shapes+=[((4,2,BS,BS),BF)]*8

    def kernel(*refs):
        attend_kernel(first,*refs)

    return pl.pallas_call(
        kernel,
        out_shape=tuple(jax.ShapeDtypeStruct(*s) for s in shapes),
        in_specs=specs,
        out_specs=(VM,)*len(shapes),
        scratch_shapes=[pltpu.VMEM((8,G*BS,2*BS),F32),pltpu.VMEM((8,G*BS,2*BS),BF)]
        +[pltpu.VMEM((G*BS,BS),F32)]*4
        +[pltpu.VMEM((G*BS,BS),BF),pltpu.VMEM((BS,G*BS),BF)]*2
        +[pltpu.VMEM((32,2,BS,BS),BF),pltpu.SemaphoreType.DMA((8,))],
        input_output_aliases={} if first else {13:3},
        compiler_params=pltpu.CompilerParams(vmem_limit_bytes=20<<20),
        cost_estimate=pl.CostEstimate(flops=10_000_000_000,bytes_accessed=24<<20,transcendentals=4<<20),
        name="attend_blocks",
    )(*args)


def join_kernel(own,far,sel,k_out,v_out):
    for w,out in ((0,k_out),(1,v_out)):
        for b in range(2):
            both=jnp.concatenate([own[b,w].T,far[b,w].T],1)
            full=dot(both,sel[...],NT).astype(BF)
            out[0,b*BS:(b+1)*BS,:]=full[:,:BS]
            out[1,b*BS:(b+1)*BS,:]=full[:,BS:]


def unite_kernel(q,g,back,sel,q_out,g_out):
    for w,mine,out in ((0,q,q_out),(1,g,g_out)):
        for b in range(2):
            both=jnp.concatenate([mine[b],back[w,b]],1)
            full=dot(both,sel[...],NT).astype(BF)
            out[0,b*BS:(b+1)*BS,:]=full[:,:BS]
            out[1,b*BS:(b+1)*BS,:]=full[:,BS:]


def small_call(kernel,*args):
    VM=pl.BlockSpec(memory_space=pltpu.VMEM)
    return pl.pallas_call(
        kernel,
        out_shape=(jax.ShapeDtypeStruct((2,2*BS,BS),BF),)*2,
        in_specs=[VM]*len(args),
        out_specs=(VM,)*2,
        compiler_params=pltpu.CompilerParams(vmem_limit_bytes=8<<20),
        cost_estimate=pl.CostEstimate(flops=1<<28,bytes_accessed=1<<20,transcendentals=0),
    )(*args)


def to_col(x,dy,dx,dc):
    pairs=[]
    for s in range(16):
        sy,sx,sc=s//4,(s//2)%2,s%2
        pairs.append((s,((sy+dy)%4)*4+(sx^dx)*2+(sc^dc)))
    return lax.ppermute(x,"col",pairs)


def to_row(x,dx,dz):
    pairs=[(s,((s//4)^dx)*4+(s%4+dz)%4) for s in range(8)]
    return lax.ppermute(x,"row",pairs)


def cross(x):
    pairs=[]
    for r in range(8):
        for c in range(16):
            pairs.append((r*16+c,(r^4)*16+(c^1)))
    return lax.ppermute(x,("row","col"),pairs)


def swap(x):
    return to_col(x,0,0,1)


def plus(*terms):
    total=terms[0].astype(F32)
    for t in terms[1:]:
        total=total+t.astype(F32)
    return total


def body(
    query_vectors,
    key_vectors,
    value_vectors,
    gate_logits,
    cotangent,
    pair_bias,
    block_table,
    valid_counts,
):
    col=lax.axis_index("col")
    row=lax.axis_index("row")
    y,xl,core=col//4,(col//2)%2,col%2
    xh,z=row//4,row%4

    src=lax.broadcasted_iota(jnp.int32,(256,256),0)
    dst=lax.broadcasted_iota(jnp.int32,(256,256),1)
    want=((dst%BS)//64)*BS+((dst//BS)^core)*64+dst%64
    sel=lax.optimization_barrier((src==want).astype(BF))

    def split(x):
        both=lax.dot_general(x.reshape(2*BS,2*BS),sel,NN,preferred_element_type=F32).astype(BF)
        return both[:,:BS].reshape(2,BS,BS),both[:,BS:].reshape(2,BS,BS)

    k_mine,k_send=split(key_vectors)
    v_mine,v_send=split(value_vectors)
    shard=jnp.concatenate([jnp.stack([k_mine,v_mine],1),swap(jnp.stack([k_send,v_send],1))],0)
    shard,pair_bias=lax.optimization_barrier((shard,pair_bias))

    def gather(x,dy,dx):
        return to_col(x,(4-dy)%4,dx,0)

    near=gather(shard,0,1)
    up,down,across=gather(shard,1,0),gather(shard,3,0),gather(shard,2,0)
    pieces=[shard, near, up, gather(near,1,0), across, gather(across,0,1), down, gather(near,3,0)]

    table=jnp.concatenate([block_table,valid_counts[:,None]],1)
    tables=[table,swap(table)]

    def places(t):
        ids=t[:,:TAB]
        owner=ids//2
        chip=((owner//4-y)%4)*2+(((owner//2)%2)^xl)
        return chip*4+((owner%2)^core)*2+ids%2

    dest=jnp.arange(8,dtype=jnp.int32)
    far=(dest//4)^xh
    turn=(dest%4-z)%4

    bias=pair_bias.transpose(0,1,3,2,4)
    bias_mine=lax.dynamic_slice_in_dim(bias,2*core,2,1)
    bias_other=swap(lax.dynamic_slice_in_dim(bias,2-2*core,2,1))
    parts=[split(x) for x in (query_vectors,gate_logits,cotangent)]
    mine=jnp.stack([p[0] for p in parts],0)
    other=swap(jnp.stack([p[1] for p in parts],0))

    ready=(places(tables[0]),tables[0][:,TAB],places(tables[1]),tables[1][:,TAB],mine,other,bias_mine,bias_other,pieces)
    idx0,cnt0,idx1,cnt1,mine,other,bias_mine,bias_other,pieces=lax.optimization_barrier(ready)
    by_z,by_x=turn*2+far,far*4+turn

    def row_sums(x):
        out=[x[0]]
        for dz in range(1,4):
            out.append(to_row(x[dz],0,dz))
        return plus(*out)

    def step(x,dy,dx):
        return to_col(x,dy,dx,0)

    dq1,gg1,bg1,acc=attend_blocks(idx1,cnt1,by_z[None],other,bias_other,pieces,None)
    q_back=swap(jnp.stack([dq1,gg1],0))
    bg1=row_sums(bg1.reshape(4,2,2,2,2,BS,BS)).astype(BF)
    dq0,gg0,bg0,_,*t=attend_blocks(
        idx0,cnt0,jnp.stack([by_z,by_x],0),mine,bias_mine,pieces,acc
    )

    straight=bg0[0].reshape(4,2,2,2,BS,BS)
    turned=bg0[1].reshape(2,4,2,2,BS,BS)
    turned_in=to_row(turned[1],1,0)
    straight=row_sums(straight).astype(BF)
    turned=plus(turned[0],turned_in).astype(BF)
    up=step(jnp.stack([t[2],t[3]],0),1,0)
    down=step(jnp.stack([t[6],t[7]],0),3,0)
    near=step(t[5],0,1)
    steps=[up[0],down[0]]
    side=plus(t[1],up[1],down[1]).astype(BF)
    over=plus(t[4],near).astype(BF)
    steps+=[step(side,0,1),step(over,2,0)]
    bias_far=cross(bg1[1])
    bias_near=swap(bg1[0])
    bias_other=plus(bias_near,bias_far).astype(BF)
    straight_in=to_row(straight[1],1,0)
    straight=plus(straight[0],straight_in).astype(BF)
    turned=row_sums(turned).astype(BF)

    query_grad,gate_grad=small_call(unite_kernel,dq0,gg0,q_back,sel)
    own=plus(t[0],*steps)
    own=jnp.stack([own[:,0]*SCALE,own[:,1]],1).astype(BF)
    own_far=swap(own[2:])
    key_grad,value_grad=small_call(join_kernel,own[:2],own_far,sel)

    bias_own=jnp.stack([straight,turned],0)
    low=jnp.where(core==0,bias_own,bias_other)
    high=jnp.where(core==0,bias_other,bias_own)
    bias_grad=jnp.concatenate([low,high],1).transpose(0,1,3,2,4)

    def rows(x):
        return x.transpose(1,0,2)

    return rows(query_grad),rows(key_grad),rows(value_grad),rows(gate_grad),bias_grad


def solution(mesh):
    return jax.shard_map(
        body,
        mesh=mesh,
        in_specs=(
            P("col","row",None),
            P("col","row",None),
            P("col","row",None),
            P("col","row",None),
            P("col","row",None),
            P("col",None,None,None,None),
            P("col",None),
            P("col"),
        ),
        out_specs=(
            P("col","row",None),
            P("col","row",None),
            P("col","row",None),
            P("col","row",None),
            P("col",None,None,"row",None),
        ),
        check_vma=False,
    )
```

```python
import math

import jax
import jax.numpy as jnp
from jax import lax
from jax.experimental import pallas as pl
from jax.experimental.pallas import tpu as pltpu
from jax.sharding import PartitionSpec as P


DH,BS,TAB=32,128,16
G=4
SCALE=DH**-0.5
LOG2E=math.log2(math.e)
F32=jnp.float32
BF=jnp.bfloat16
NT=(((1,),(1,)),((),()))
NN=(((1,),(0,)),((),()))


def dot(a,b,dims): return lax.dot_general(a,b,dims,preferred_element_type=F32)


def loop2(pairs,f):
    def two(k,c):
        f(2*k,0); f(2*k+1,0)
        return c
    def four(k,c):
        for u in range(4):
            f(4*k+u,0)
        return c
    lax.fori_loop(0,pairs//4,four,0)
    @pl.when(pairs%4>=2)
    def _():
        two(pairs//4*2,0)
    @pl.when(pairs%2==1)
    def _(): f(pairs-1,0)


def attend_kernel(first,*refs):
    idx,cnt,chk,qgc,bias=refs[:5]
    q,gate,cot=qgc.at[0],qgc.at[1],qgc.at[2]
    pieces=refs[5:13]
    if first:
        dq,gg,bg,acc=refs[13:17]
        rest=refs[17:]
    else:
        dq,gg,bg,acc=refs[14:18]
        terms=refs[18:24]
        rest=refs[24:]
    s_ref,e_ref,m_ref,l_ref,o_ref,off_ref,qm,qt,dom,domt,kv,sem=rest
    for m in range(8):
        pltpu.make_async_copy(pieces[m],kv.at[pl.ds(4*m,4)],sem.at[m]).start()
    lane=lax.broadcasted_iota(jnp.int32,(BS,BS),1)//DH
    chan=lax.broadcasted_iota(jnp.int32,(BS,BS),0)//DH
    if first:
        acc[...]=jnp.zeros(acc.shape,F32)
    for m in range(8):
        pltpu.make_async_copy(pieces[m],kv.at[pl.ds(4*m,4)],sem.at[m]).wait()

    def spot(j,p,h):
        if first:
            return chk[0,p]*4+2*j+h
        if h==0:
            return chk[0,p]*3+2*j
        return jnp.where(j==0,chk[0,p]*3+1,24+chk[1,p])

    def block(j,carry):
        n=cnt[j]
        pairs=(n+1)//2
        qj=q[j]
        qj_t=qj.T
        for g in range(G):
            r=slice(g*BS,(g+1)*BS)
            qm[r,:]=jnp.where(lane==g,qj,jnp.zeros_like(qj))
            qt[:,r]=jnp.where(chan==g,qj_t,jnp.zeros_like(qj_t))
        m_ref[...]=jnp.full(m_ref.shape,-jnp.inf,F32)
        l_ref[...]=jnp.zeros(l_ref.shape,F32)
        o_ref[...]=jnp.zeros(o_ref.shape,F32)
        def both(p,w):
            return jnp.concatenate([kv[idx[j,2*p],w],kv[idx[j,2*p+1],w]],0)
        def score(p,c):
            k2=both(p,0)
            S=dot(qm[...],k2,NT)*(SCALE*LOG2E)
            for h in range(2):
                b0=bias[j,h,2*p].astype(F32)*LOG2E
                b1=bias[j,h,2*p+1].astype(F32)*LOG2E
                b1=jnp.where(2*p+1<n,b1,-1e30)
                for i in range(2):
                    g=2*i+h
                    r=slice(g*BS,(g+1)*BS)
                    s=S[r,:]
                    s0=s[:,:BS]+b0; s1=s[:,BS:]+b1
                    s_ref[p,r,:BS]=s0
                    s_ref[p,r,BS:]=s1
                    m_ref[r,:]=jnp.maximum(m_ref[r,:],jnp.maximum(s0,s1))
            return c
        loop2(pairs,score)
        m_ref[...]=jnp.broadcast_to(jnp.max(m_ref[...],axis=1,keepdims=True),m_ref.shape)
        def attend(p,c):
            v2=both(p,1)
            for g in range(G):
                r=slice(g*BS,(g+1)*BS)
                m=m_ref[r,:]
                e0=jnp.exp2(s_ref[p,r,:BS]-m); e1=jnp.exp2(s_ref[p,r,BS:]-m)
                l_ref[r,:]+=e0+e1
                e=jnp.concatenate([e0.astype(BF),e1.astype(BF)],1)
                e_ref[p,r,:]=e
            o_ref[...]+=dot(e_ref[p],v2,NN)
            return c
        loop2(pairs,attend)
        att=jnp.zeros((BS,BS),F32)
        inv=jnp.zeros((BS,BS),F32)
        for g in range(G):
            r=slice(g*BS,(g+1)*BS)
            one=1.0/jnp.sum(l_ref[r,:],axis=1,keepdims=True)
            att=jnp.where(lane==g,o_ref[r,:],att)
            inv=jnp.where(lane==g,one,inv)
        att=att*inv
        c=cot[j].astype(F32)
        opened=1.0/(1.0+jnp.exp(-gate[j].astype(F32)))
        gg[j]=(c*att*opened*(1.0-opened)).astype(BF)
        d=((c*opened).astype(BF).astype(F32)*inv).astype(BF)
        d_t=d.T
        x=d.astype(F32)*att
        for g in range(G):
            r=slice(g*BS,(g+1)*BS)
            dom[r,:]=jnp.where(lane==g,d,jnp.zeros_like(d))
            domt[:,r]=jnp.where(chan==g,d_t,jnp.zeros_like(d_t))
            off=jnp.sum(jnp.where(lane==g,x,0.0),axis=1,keepdims=True)
            off_ref[r,:]=jnp.broadcast_to(off,(BS,BS))
        o_ref[...]=jnp.zeros(o_ref.shape,F32)
        def backward(p,c):
            a0=idx[j,2*p]; a1=idx[j,2*p+1]
            spots=[spot(j,p,h) for h in range(2)]
            k2=both(p,0); v2=both(p,1)
            halves=[]; total=[None,None]
            WG=dot(dom[...],v2,NT)
            for g in range(G):
                r=slice(g*BS,(g+1)*BS); h=g%2
                off=off_ref[r,:]
                wg=WG[r,:]
                ds=e_ref[p,r,:].astype(F32)*(wg-jnp.concatenate([off,off],1))
                if g<2: total[h]=ds
                else:
                    b=(total[h]+ds).astype(BF)
                    bg[spots[h],0]=b[:,:BS]; bg[spots[h],1]=b[:,BS:]
                half=ds.astype(BF)
                halves.append(half)
            hs=jnp.concatenate(halves,0)
            o_ref[...]+=dot(hs,k2,NN)
            dk=dot(qt[...],hs,NN)
            dv=dot(domt[...],e_ref[p],NN)
            acc[a0,0]+=dk[:,:BS]; acc[a1,0]+=dk[:,BS:]
            acc[a0,1]+=dv[:,:BS]; acc[a1,1]+=dv[:,BS:]
            return c
        loop2(pairs,backward)
        def clear(p,c):
            for h in range(2):
                bg[spot(j,p,h)]=jnp.zeros((2,BS,BS),BF)
            return c
        lax.fori_loop(pairs,8,clear,0)
        x=jnp.zeros((BS,BS),F32)
        for g in range(G):
            x=jnp.where(lane==g,o_ref[g*BS:(g+1)*BS,:],x)
        dq[j]=(x*SCALE).astype(BF)
        return carry
    lax.fori_loop(0,2,block,0)
    if not first:
        for out,m in zip(terms,(0,1,2,4,5,6)):
            out[...]=acc[4*m:4*m+out.shape[0]].astype(BF)


def attend_blocks(idx,cnt,chk,qgc,bias,pieces,prev):
    first=prev is None
    SM=pl.BlockSpec(memory_space=pltpu.SMEM)
    VM=pl.BlockSpec(memory_space=pltpu.VMEM)
    AN=pl.BlockSpec(memory_space=pl.ANY)
    args=[idx,cnt,chk,qgc,bias,*pieces]
    specs=[SM]*3+[VM]*2+[AN]*8
    shapes=[((2,BS,BS),BF),((2,BS,BS),BF),((32,2,BS,BS),BF),((32,2,BS,BS),F32)]
    if not first:
        args.append(prev)
        specs.append(VM)
        shapes+=[((n,2,BS,BS),BF) for n in (4,4,8,4,4,8)]

    def kernel(*refs):
        attend_kernel(first,*refs)

    return pl.pallas_call(
        kernel,
        out_shape=tuple(jax.ShapeDtypeStruct(*s) for s in shapes),
        in_specs=specs,
        out_specs=(VM,)*len(shapes),
        scratch_shapes=[pltpu.VMEM((8,G*BS,2*BS),F32),pltpu.VMEM((8,G*BS,2*BS),BF)]
        +[pltpu.VMEM((G*BS,BS),F32)]*4
        +[pltpu.VMEM((G*BS,BS),BF),pltpu.VMEM((BS,G*BS),BF)]*2
        +[pltpu.VMEM((32,2,BS,BS),BF),pltpu.SemaphoreType.DMA((8,))],
        input_output_aliases={} if first else {13:3},
        compiler_params=pltpu.CompilerParams(vmem_limit_bytes=20<<20),
        cost_estimate=pl.CostEstimate(flops=10_000_000_000,bytes_accessed=24<<20,transcendentals=4<<20),
        name="attend_blocks",
    )(*args)


def join_kernel(own,far,sel,k_out,v_out):
    for w,out in ((0,k_out),(1,v_out)):
        for b in range(2):
            both=jnp.concatenate([own[b,w].T,far[b,w].T],1)
            full=dot(both,sel[...],NT).astype(BF)
            out[0,b*BS:(b+1)*BS,:]=full[:,:BS]
            out[1,b*BS:(b+1)*BS,:]=full[:,BS:]


def unite_kernel(q,g,back,sel,q_out,g_out):
    for w,mine,out in ((0,q,q_out),(1,g,g_out)):
        for b in range(2):
            both=jnp.concatenate([mine[b],back[w,b]],1)
            full=dot(both,sel[...],NT).astype(BF)
            out[0,b*BS:(b+1)*BS,:]=full[:,:BS]
            out[1,b*BS:(b+1)*BS,:]=full[:,BS:]


def small_call(kernel,*args):
    VM=pl.BlockSpec(memory_space=pltpu.VMEM)
    return pl.pallas_call(
        kernel,
        out_shape=(jax.ShapeDtypeStruct((2,2*BS,BS),BF),)*2,
        in_specs=[VM]*len(args),
        out_specs=(VM,)*2,
        compiler_params=pltpu.CompilerParams(vmem_limit_bytes=8<<20),
        cost_estimate=pl.CostEstimate(flops=1<<28,bytes_accessed=1<<20,transcendentals=0),
    )(*args)


def to_col(x,dy,dx,dc):
    pairs=[]
    for s in range(16):
        sy,sx,sc=s//4,(s//2)%2,s%2
        pairs.append((s,((sy+dy)%4)*4+(sx^dx)*2+(sc^dc)))
    return lax.ppermute(x,"col",pairs)


def to_row(x,dx,dz):
    pairs=[(s,((s//4)^dx)*4+(s%4+dz)%4) for s in range(8)]
    return lax.ppermute(x,"row",pairs)


def cross(x):
    pairs=[]
    for r in range(8):
        for c in range(16):
            pairs.append((r*16+c,(r^4)*16+(c^1)))
    return lax.ppermute(x,("row","col"),pairs)


def swap(x):
    return to_col(x,0,0,1)


def plus(*terms):
    total=terms[0].astype(F32)
    for t in terms[1:]:
        total=total+t.astype(F32)
    return total


def body(
    query_vectors,
    key_vectors,
    value_vectors,
    gate_logits,
    cotangent,
    pair_bias,
    block_table,
    valid_counts,
):
    col=lax.axis_index("col")
    row=lax.axis_index("row")
    y,xl,core=col//4,(col//2)%2,col%2
    xh,z=row//4,row%4

    src=lax.broadcasted_iota(jnp.int32,(256,256),0)
    dst=lax.broadcasted_iota(jnp.int32,(256,256),1)
    want=((dst%BS)//64)*BS+((dst//BS)^core)*64+dst%64
    sel=lax.optimization_barrier((src==want).astype(BF))

    def split(x):
        both=lax.dot_general(x.reshape(2*BS,2*BS),sel,NN,preferred_element_type=F32).astype(BF)
        return both[:,:BS].reshape(2,BS,BS),both[:,BS:].reshape(2,BS,BS)

    k_mine,k_send=split(key_vectors)
    v_mine,v_send=split(value_vectors)
    shard=jnp.concatenate([jnp.stack([k_mine,v_mine],1),swap(jnp.stack([k_send,v_send],1))],0)
    shard,pair_bias=lax.optimization_barrier((shard,pair_bias))
    def gather(x,dy,dx):
        return to_col(x,(4-dy)%4,dx,0)

    near=gather(shard,0,1)
    up,down,across=gather(shard,1,0),gather(shard,3,0),gather(shard,2,0)
    pieces=[shard, near, up, gather(near,1,0), across, gather(across,0,1), down, gather(near,3,0)]

    table=jnp.concatenate([block_table,valid_counts[:,None]],1)
    tables=[table,swap(table)]

    def places(t):
        ids=t[:,:TAB]
        owner=ids//2
        chip=((owner//4-y)%4)*2+(((owner//2)%2)^xl)
        return chip*4+((owner%2)^core)*2+ids%2

    dest=jnp.arange(8,dtype=jnp.int32)
    far=(dest//4)^xh
    turn=(dest%4-z)%4

    bias=pair_bias.transpose(0,1,3,2,4)
    bias_mine=lax.dynamic_slice_in_dim(bias,2*core,2,1)
    bias_other=swap(lax.dynamic_slice_in_dim(bias,2-2*core,2,1))
    parts=[split(x) for x in (query_vectors,gate_logits,cotangent)]
    mine=jnp.stack([p[0] for p in parts],0)
    other=swap(jnp.stack([p[1] for p in parts],0))

    ready=(places(tables[0]),tables[0][:,TAB],places(tables[1]),tables[1][:,TAB],mine,other,bias_mine,bias_other,pieces)
    idx0,cnt0,idx1,cnt1,mine,other,bias_mine,bias_other,pieces=lax.optimization_barrier(ready)
    by_z,by_x=turn*2+far,far*4+turn

    def row_sums(x):
        out=[x[0]]
        for dz in range(1,4):
            out.append(to_row(x[dz],0,dz))
        return plus(*out)

    def step(x,dy,dx):
        return to_col(x,dy,dx,0)

    dq1,gg1,bg1,acc=attend_blocks(idx1,cnt1,by_z[None],other,bias_other,pieces,None)
    bg1=row_sums(bg1.reshape(4,2,2,2,2,BS,BS)).astype(BF)
    second=jnp.stack([by_z,by_x],0)
    dq0,gg0,bg0,_,*t=attend_blocks(
        idx0,cnt0,second,mine,bias_mine,pieces,acc
    )

    straight=bg0[:24].reshape(4,2,3,2,BS,BS)
    turned=bg0[24:].reshape(2,4,2,BS,BS)
    turned_in=to_row(turned[1],1,0)
    straight=row_sums(straight).astype(BF)
    turned=plus(turned[0],turned_in).astype(BF)
    t00,t01,t1,t20,t21,t3=t
    up=step(t1,1,0)
    down=step(t3,3,0)
    near=step(t21,0,1)
    steps=[up[:4],down[:4]]
    side=plus(t01,up[4:],down[4:]).astype(BF)
    over=plus(t20,near).astype(BF)
    steps+=[step(side,0,1),step(over,2,0)]
    bias_far=cross(bg1[1])
    bias_near=swap(bg1[0])
    bias_other=plus(bias_near,bias_far).astype(BF)
    straight_in=to_row(straight[1],1,0)
    straight=plus(straight[0],straight_in).astype(BF)
    turned=row_sums(turned).astype(BF)

    q_back=swap(jnp.stack([dq1,gg1],0))
    query_grad,gate_grad=small_call(unite_kernel,dq0,gg0,q_back,sel)
    own=plus(t00,*steps)
    own=jnp.stack([own[:,0]*SCALE,own[:,1]],1).astype(BF)
    own_far=swap(own[2:])
    key_grad,value_grad=small_call(join_kernel,own[:2],own_far,sel)

    bias_own=jnp.concatenate([straight,turned[None]],0).reshape(2,2,2,BS,BS)
    low=jnp.where(core==0,bias_own,bias_other)
    high=jnp.where(core==0,bias_other,bias_own)
    bias_grad=jnp.concatenate([low,high],1).transpose(0,1,3,2,4)

    def rows(x):
        return x.transpose(1,0,2)

    return rows(query_grad),rows(key_grad),rows(value_grad),rows(gate_grad),bias_grad


def solution(mesh):
    return jax.shard_map(
        body,
        mesh=mesh,
        in_specs=(
            P("col","row",None),
            P("col","row",None),
            P("col","row",None),
            P("col","row",None),
            P("col","row",None),
            P("col",None,None,None,None),
            P("col",None),
            P("col"),
        ),
        out_specs=(
            P("col","row",None),
            P("col","row",None),
            P("col","row",None),
            P("col","row",None),
            P("col",None,None,"row",None),
        ),
        check_vma=False,
    )
```

```python
import math

import jax
import jax.numpy as jnp
from jax import lax
from jax.experimental import pallas as pl
from jax.experimental.pallas import tpu as pltpu
from jax.sharding import PartitionSpec as P


DH,BS,TAB=32,128,16
G=4
SCALE=DH**-0.5
LOG2E=math.log2(math.e)
F32=jnp.float32
BF=jnp.bfloat16
NT=(((1,),(1,)),((),()))
NN=(((1,),(0,)),((),()))


def dot(a,b,dims): return lax.dot_general(a,b,dims,preferred_element_type=F32)


def loop2(pairs,f):
    def two(k,c):
        f(2*k,0); f(2*k+1,0)
        return c
    def four(k,c):
        for u in range(4):
            f(4*k+u,0)
        return c
    lax.fori_loop(0,pairs//4,four,0)
    @pl.when(pairs%4>=2)
    def _():
        two(pairs//4*2,0)
    @pl.when(pairs%2==1)
    def _(): f(pairs-1,0)


def attend_kernel(first,*refs):
    idx,cnt,chk,qgc,bias=refs[:5]
    q,gate,cot=qgc.at[0],qgc.at[1],qgc.at[2]
    pieces=refs[5:13]
    if first:
        dq,gg,bg,acc=refs[13:17]
        rest=refs[17:]
    else:
        dq,gg,bg,acc=refs[14:18]
        terms=refs[18:24]
        rest=refs[24:]
    s_ref,e_ref,m_ref,l_ref,o_ref,off_ref,qm,qt,dom,domt,kv,sem=rest
    for m in range(8):
        pltpu.make_async_copy(pieces[m],kv.at[pl.ds(4*m,4)],sem.at[m]).start()
    lane=lax.broadcasted_iota(jnp.int32,(BS,BS),1)//DH
    chan=lax.broadcasted_iota(jnp.int32,(BS,BS),0)//DH
    if first:
        acc[...]=jnp.zeros(acc.shape,F32)
    for m in range(8):
        pltpu.make_async_copy(pieces[m],kv.at[pl.ds(4*m,4)],sem.at[m]).wait()

    def block(j,carry):
        n=cnt[j]
        pairs=(n+1)//2
        qj=q[j]
        qj_t=qj.T
        for g in range(G):
            r=slice(g*BS,(g+1)*BS)
            qm[r,:]=jnp.where(lane==g,qj,jnp.zeros_like(qj))
            qt[:,r]=jnp.where(chan==g,qj_t,jnp.zeros_like(qj_t))
        m_ref[...]=jnp.full(m_ref.shape,-jnp.inf,F32)
        l_ref[...]=jnp.zeros(l_ref.shape,F32)
        o_ref[...]=jnp.zeros(o_ref.shape,F32)
        def both(p,w):
            return jnp.concatenate([kv[idx[j,2*p],w],kv[idx[j,2*p+1],w]],0)
        def score(p,c):
            k2=both(p,0)
            S=dot(qm[...],k2,NT)*(SCALE*LOG2E)
            for h in range(2):
                b0=bias[j,h,2*p].astype(F32)*LOG2E
                b1=bias[j,h,2*p+1].astype(F32)*LOG2E
                b1=jnp.where(2*p+1<n,b1,-1e30)
                for i in range(2):
                    g=2*i+h
                    r=slice(g*BS,(g+1)*BS)
                    s=S[r,:]
                    s0=s[:,:BS]+b0; s1=s[:,BS:]+b1
                    s_ref[p,r,:BS]=s0
                    s_ref[p,r,BS:]=s1
                    m_ref[r,:]=jnp.maximum(m_ref[r,:],jnp.maximum(s0,s1))
            return c
        loop2(pairs,score)
        m_ref[...]=jnp.broadcast_to(jnp.max(m_ref[...],axis=1,keepdims=True),m_ref.shape)
        def attend(p,c):
            v2=both(p,1)
            for g in range(G):
                r=slice(g*BS,(g+1)*BS)
                m=m_ref[r,:]
                e0=jnp.exp2(s_ref[p,r,:BS]-m); e1=jnp.exp2(s_ref[p,r,BS:]-m)
                l_ref[r,:]+=e0+e1
                e=jnp.concatenate([e0.astype(BF),e1.astype(BF)],1)
                e_ref[p,r,:]=e
            o_ref[...]+=dot(e_ref[p],v2,NN)
            return c
        loop2(pairs,attend)
        att=jnp.zeros((BS,BS),F32)
        inv=jnp.zeros((BS,BS),F32)
        for g in range(G):
            r=slice(g*BS,(g+1)*BS)
            one=1.0/jnp.sum(l_ref[r,:],axis=1,keepdims=True)
            att=jnp.where(lane==g,o_ref[r,:],att)
            inv=jnp.where(lane==g,one,inv)
        att=att*inv
        c=cot[j].astype(F32)
        opened=1.0/(1.0+jnp.exp(-gate[j].astype(F32)))
        gg[j]=(c*att*opened*(1.0-opened)).astype(BF)
        d=((c*opened).astype(BF).astype(F32)*inv).astype(BF)
        d_t=d.T
        x=d.astype(F32)*att
        for g in range(G):
            r=slice(g*BS,(g+1)*BS)
            dom[r,:]=jnp.where(lane==g,d,jnp.zeros_like(d))
            domt[:,r]=jnp.where(chan==g,d_t,jnp.zeros_like(d_t))
            off=jnp.sum(jnp.where(lane==g,x,0.0),axis=1,keepdims=True)
            off_ref[r,:]=jnp.broadcast_to(off,(BS,BS))
        o_ref[...]=jnp.zeros(o_ref.shape,F32)
        def backward(p,c):
            a0=idx[j,2*p]; a1=idx[j,2*p+1]
            out=bg.at[chk[0,p],j] if first else bg.at[j,chk[j,p]]
            k2=both(p,0); v2=both(p,1)
            halves=[]; total=[None,None]
            WG=dot(dom[...],v2,NT)
            for g in range(G):
                r=slice(g*BS,(g+1)*BS); h=g%2
                off=off_ref[r,:]
                wg=WG[r,:]
                ds=e_ref[p,r,:].astype(F32)*(wg-jnp.concatenate([off,off],1))
                if g<2: total[h]=ds
                else:
                    b=(total[h]+ds).astype(BF)
                    out[h,0]=b[:,:BS]; out[h,1]=b[:,BS:]
                half=ds.astype(BF)
                halves.append(half)
            hs=jnp.concatenate(halves,0)
            o_ref[...]+=dot(hs,k2,NN)
            dk=dot(qt[...],hs,NN)
            dv=dot(domt[...],e_ref[p],NN)
            acc[a0,0]+=dk[:,:BS]; acc[a1,0]+=dk[:,BS:]
            acc[a0,1]+=dv[:,:BS]; acc[a1,1]+=dv[:,BS:]
            return c
        loop2(pairs,backward)
        def clear(p,c):
            out=bg.at[chk[0,p],j] if first else bg.at[j,chk[j,p]]
            out[...]=jnp.zeros((2,2,BS,BS),BF)
            return c
        lax.fori_loop(pairs,8,clear,0)
        x=jnp.zeros((BS,BS),F32)
        for g in range(G):
            x=jnp.where(lane==g,o_ref[g*BS:(g+1)*BS,:],x)
        dq[j]=(x*SCALE).astype(BF)
        return carry
    lax.fori_loop(0,2,block,0)
    if not first:
        for out,m in zip(terms,(0,1,2,4,5,6)):
            out[...]=acc[4*m:4*m+out.shape[0]].astype(BF)


def attend_blocks(idx,cnt,chk,qgc,bias,pieces,prev):
    first=prev is None
    SM=pl.BlockSpec(memory_space=pltpu.SMEM)
    VM=pl.BlockSpec(memory_space=pltpu.VMEM)
    AN=pl.BlockSpec(memory_space=pl.ANY)
    args=[idx,cnt,chk,qgc,bias,*pieces]
    specs=[SM]*3+[VM]*2+[AN]*8
    lead=(8,2) if first else (2,8)
    shapes=[((2,BS,BS),BF),((2,BS,BS),BF),(lead+(2,2,BS,BS),BF),((32,2,BS,BS),F32)]
    if not first:
        args.append(prev)
        specs.append(VM)
        shapes+=[((n,2,BS,BS),BF) for n in (4,4,8,4,4,8)]

    def kernel(*refs):
        attend_kernel(first,*refs)

    return pl.pallas_call(
        kernel,
        out_shape=tuple(jax.ShapeDtypeStruct(*s) for s in shapes),
        in_specs=specs,
        out_specs=(VM,)*len(shapes),
        scratch_shapes=[pltpu.VMEM((8,G*BS,2*BS),F32),pltpu.VMEM((8,G*BS,2*BS),BF)]
        +[pltpu.VMEM((G*BS,BS),F32)]*4
        +[pltpu.VMEM((G*BS,BS),BF),pltpu.VMEM((BS,G*BS),BF)]*2
        +[pltpu.VMEM((32,2,BS,BS),BF),pltpu.SemaphoreType.DMA((8,))],
        input_output_aliases={} if first else {13:3},
        compiler_params=pltpu.CompilerParams(vmem_limit_bytes=20<<20),
        cost_estimate=pl.CostEstimate(flops=10_000_000_000,bytes_accessed=24<<20,transcendentals=4<<20),
        name="attend_blocks",
    )(*args)


def join_kernel(own,far,sel,k_out,v_out):
    for w,out in ((0,k_out),(1,v_out)):
        for b in range(2):
            both=jnp.concatenate([own[b,w].T,far[b,w].T],1)
            full=dot(both,sel[...],NT).astype(BF)
            out[0,b*BS:(b+1)*BS,:]=full[:,:BS]
            out[1,b*BS:(b+1)*BS,:]=full[:,BS:]


def unite_kernel(q,g,back,sel,q_out,g_out):
    for w,mine,out in ((0,q,q_out),(1,g,g_out)):
        for b in range(2):
            both=jnp.concatenate([mine[b],back[w,b]],1)
            full=dot(both,sel[...],NT).astype(BF)
            out[0,b*BS:(b+1)*BS,:]=full[:,:BS]
            out[1,b*BS:(b+1)*BS,:]=full[:,BS:]


def small_call(kernel,*args):
    VM=pl.BlockSpec(memory_space=pltpu.VMEM)
    return pl.pallas_call(
        kernel,
        out_shape=(jax.ShapeDtypeStruct((2,2*BS,BS),BF),)*2,
        in_specs=[VM]*len(args),
        out_specs=(VM,)*2,
        compiler_params=pltpu.CompilerParams(vmem_limit_bytes=8<<20),
        cost_estimate=pl.CostEstimate(flops=1<<28,bytes_accessed=1<<20,transcendentals=0),
    )(*args)


def to_col(x,dy,dx,dc):
    pairs=[]
    for s in range(16):
        sy,sx,sc=s//4,(s//2)%2,s%2
        pairs.append((s,((sy+dy)%4)*4+(sx^dx)*2+(sc^dc)))
    return lax.ppermute(x,"col",pairs)


def to_row(x,dx,dz):
    pairs=[(s,((s//4)^dx)*4+(s%4+dz)%4) for s in range(8)]
    return lax.ppermute(x,"row",pairs)


def cross(x):
    pairs=[]
    for r in range(8):
        for c in range(16):
            pairs.append((r*16+c,(r^4)*16+(c^1)))
    return lax.ppermute(x,("row","col"),pairs)


def swap(x):
    return to_col(x,0,0,1)


def plus(*terms):
    total=terms[0].astype(F32)
    for t in terms[1:]:
        total=total+t.astype(F32)
    return total


def body(
    query_vectors,
    key_vectors,
    value_vectors,
    gate_logits,
    cotangent,
    pair_bias,
    block_table,
    valid_counts,
):
    col=lax.axis_index("col")
    row=lax.axis_index("row")
    y,xl,core=col//4,(col//2)%2,col%2
    xh,z=row//4,row%4

    src=lax.broadcasted_iota(jnp.int32,(256,256),0)
    dst=lax.broadcasted_iota(jnp.int32,(256,256),1)
    want=((dst%BS)//64)*BS+((dst//BS)^core)*64+dst%64
    sel=lax.optimization_barrier((src==want).astype(BF))

    def split(x):
        both=lax.dot_general(x.reshape(2*BS,2*BS),sel,NN,preferred_element_type=F32).astype(BF)
        return both[:,:BS].reshape(2,BS,BS),both[:,BS:].reshape(2,BS,BS)

    k_mine,k_send=split(key_vectors)
    v_mine,v_send=split(value_vectors)
    shard=jnp.concatenate([jnp.stack([k_mine,v_mine],1),swap(jnp.stack([k_send,v_send],1))],0)
    shard,pair_bias=lax.optimization_barrier((shard,pair_bias))
    def gather(x,dy,dx):
        return to_col(x,(4-dy)%4,dx,0)

    near=gather(shard,0,1)
    up,down,across=gather(shard,1,0),gather(shard,3,0),gather(shard,2,0)
    pieces=[shard, near, up, gather(near,1,0), across, gather(across,0,1), down, gather(near,3,0)]

    table=jnp.concatenate([block_table,valid_counts[:,None]],1)
    tables=[table,swap(table)]

    def places(t):
        ids=t[:,:TAB]
        owner=ids//2
        chip=((owner//4-y)%4)*2+(((owner//2)%2)^xl)
        return chip*4+((owner%2)^core)*2+ids%2

    dest=jnp.arange(8,dtype=jnp.int32)
    far=(dest//4)^xh
    turn=(dest%4-z)%4

    bias=pair_bias.transpose(0,1,3,2,4)
    bias_mine=lax.dynamic_slice_in_dim(bias,2*core,2,1)
    bias_other=swap(lax.dynamic_slice_in_dim(bias,2-2*core,2,1))
    parts=[split(x) for x in (query_vectors,gate_logits,cotangent)]
    mine=jnp.stack([p[0] for p in parts],0)
    other=swap(jnp.stack([p[1] for p in parts],0))

    ready=(places(tables[0]),tables[0][:,TAB],places(tables[1]),tables[1][:,TAB],mine,other,bias_mine,bias_other,pieces)
    idx0,cnt0,idx1,cnt1,mine,other,bias_mine,bias_other,pieces=lax.optimization_barrier(ready)
    by_z,by_x=turn*2+far,far*4+turn

    def row_sums(x):
        out=[x[0]]
        for dz in range(1,4):
            out.append(to_row(x[dz],0,dz))
        return plus(*out)

    def step(x,dy,dx):
        return to_col(x,dy,dx,0)

    dq1,gg1,bg1,acc=attend_blocks(idx1,cnt1,by_z[None],other,bias_other,pieces,None)
    bg1=row_sums(bg1.reshape(4,2,2,2,2,BS,BS)).astype(BF)
    second=jnp.stack([by_z,by_x],0)
    dq0,gg0,bg0,_,*t=attend_blocks(
        idx0,cnt0,second,mine,bias_mine,pieces,acc
    )

    straight=bg0[0].reshape(4,2,2,2,BS,BS)
    turned=bg0[1].reshape(2,4,2,2,BS,BS)
    turned_in=to_row(turned[1],1,0)
    straight=row_sums(straight).astype(BF)
    turned=plus(turned[0],turned_in).astype(BF)
    t00,t01,t1,t20,t21,t3=t
    up=step(t1,1,0)
    down=step(t3,3,0)
    near=step(t21,0,1)
    steps=[up[:4],down[:4]]
    side=plus(t01,up[4:],down[4:]).astype(BF)
    over=plus(t20,near).astype(BF)
    steps+=[step(side,0,1),step(over,2,0)]
    bias_far=cross(bg1[1])
    bias_near=swap(bg1[0])
    bias_other=plus(bias_near,bias_far).astype(BF)
    straight_in=to_row(straight[1],1,0)
    straight=plus(straight[0],straight_in).astype(BF)
    turned=row_sums(turned).astype(BF)

    q_back=swap(jnp.stack([dq1,gg1],0))
    query_grad,gate_grad=small_call(unite_kernel,dq0,gg0,q_back,sel)
    own=plus(t00,*steps)
    own=jnp.stack([own[:,0]*SCALE,own[:,1]],1).astype(BF)
    own_far=swap(own[2:])
    key_grad,value_grad=small_call(join_kernel,own[:2],own_far,sel)

    bias_own=jnp.stack([straight,turned],0)
    low=jnp.where(core==0,bias_own,bias_other)
    high=jnp.where(core==0,bias_other,bias_own)
    bias_grad=jnp.concatenate([low,high],1).transpose(0,1,3,2,4)

    def rows(x):
        return x.transpose(1,0,2)

    return rows(query_grad),rows(key_grad),rows(value_grad),rows(gate_grad),bias_grad


def solution(mesh):
    return jax.shard_map(
        body,
        mesh=mesh,
        in_specs=(
            P("col","row",None),
            P("col","row",None),
            P("col","row",None),
            P("col","row",None),
            P("col","row",None),
            P("col",None,None,None,None),
            P("col",None),
            P("col"),
        ),
        out_specs=(
            P("col","row",None),
            P("col","row",None),
            P("col","row",None),
            P("col","row",None),
            P("col",None,None,"row",None),
        ),
        check_vma=False,
    )
```
